32 devices in a mesh: tx: 8 (over y, x, core), ty: 4 (over z).
Axes of the slice: x: 2, y: 2, z: 4, core: 2. Of those that a mesh axis runs over, the one named last changes fastest.
Arguments:
- velocity: bfloat16 [2, 60, 4, 8192], P(None, None, 'ty', 'tx'), may hold values from -6 to 6
- tracers: bfloat16 [2, 60, 4, 8192], P(None, None, 'ty', 'tx'), may hold values from -6 to 6
- surface_forcing: float32 [4, 4, 8192], P(None, 'ty', 'tx'), may hold values from -6 to 6
- thickness: float32 [60], replicated, may hold values from 0.5 to 2
- levels: int32 [4, 8192], P('ty', 'tx'), may hold values from 0 to 60, as said below
- surface_levels: int32 [128, 256], P('tx', 'ty'), may hold values from 0 to 60, as said below
- height: float32 [128, 256], P('tx', 'ty'), may hold values from -6 to 6
- transport: float32 [2, 128, 256], P(None, 'tx', 'ty'), may hold values from -12 to 12
- send_list: int32 [4, 8, 8, 128], P('ty', 'tx'), may hold values from -1 to 1023, as said below
- receive_cell: int32 [4, 8, 8, 128], P('ty', 'tx'), may hold values from -1 to 1023, as said below
- own_slot: int32 [128, 256], P('tx', 'ty'), may hold values from -1 to 1023, as said below
Outputs:
- new_velocity: bfloat16 [2, 60, 4, 8192], P(None, None, 'ty', 'tx')
- new_tracers: bfloat16 [2, 60, 4, 8192], P(None, None, 'ty', 'tx')
- new_height: float32 [128, 256], P('tx', 'ty')
- new_transport: float32 [2, 128, 256], P(None, 'tx', 'ty')
The draws below stay inside these ranges and needn't reach their ends.
Inputs may be any that keep to these rules, and one draw needn't show every extreme that they name: levels and surface_levels describe one bathymetry: a slot's count equals that of its surface cell; 0 marks land. `surface_levels`: the same bathymetry as levels. send_list[j, i, d] lists distinct slots of tx index i, then -1; none for d = i; every pair i != d has at least one and at most 128 entries, exactly 128 for some pair in each tile column; as many columns go from i to d as from d to i; each slot is listed once or named by own_slot. receive_cell[j, d, i] holds as many entries as send_list[j, i, d], the cells of those columns in the same order, then -1; every cell of an area tile is named once here or has own_slot >= 0. `own_slot`: -1 where the column lies on another device.
All inputs are finite; a program needn't handle non-finite values.
Results may differ from the reference program's by a relative error of at most 0.001.
Values sent between devices are 32-bit elements; how exact they have to be, the bound alone decides.
A program may use at most 64 MiB of HBM per device.

```python
import math
import jax
import jax.numpy as jnp
from jax import lax

LEV = 60
AY = 64
NSUB = 16
STEPS = 2
COLS = 1024
CAP = 128
NXG = 128
NYG = 256
VCOLS = 8192
N_TX = 8
N_TY = 4


def layout(key):
    cells = N_TX * COLS
    streams = [jax.random.fold_in(key, 7001 + number) for number in range(7)]
    depth_draw = jax.random.randint(streams[0], (N_TY, cells), 1, LEV + 1)
    land = jax.random.randint(streams[1], (N_TY, cells), 0, 4) == 0
    bathymetry = jnp.where(land, 0, depth_draw).astype(jnp.int32)
    raw = jax.random.randint(streams[2], (N_TY, N_TX, N_TX), 1, CAP + 1).astype(jnp.int32)
    upper_part = jnp.triu(raw, 1)
    amounts = upper_part + jnp.swapaxes(upper_part, 1, 2)
    first = jax.random.randint(streams[3], (N_TY,), 0, N_TX)
    second = (first + jax.random.randint(streams[4], (N_TY,), 1, N_TX)) % N_TX
    index = jnp.arange(N_TX)
    chosen = (index[None, :, None] == first[:, None, None]) & (index[None, None, :] == second[:, None, None]) | (index[None, :, None] == second[:, None, None]) & (index[None, None, :] == first[:, None, None])
    amounts = jnp.where(chosen, CAP, amounts).astype(jnp.int32)
    kept = COLS - jnp.sum(amounts, axis=2)
    counts = (amounts + jnp.eye(N_TX, dtype=jnp.int32)[None] * kept[:, :, None]).astype(jnp.int32)
    cell_keys = jax.random.split(streams[5], N_TY * N_TX)
    cell_order = jax.vmap(lambda item: jax.random.permutation(item, COLS))(cell_keys).reshape(N_TY, N_TX, COLS).astype(jnp.int32)
    slot_keys = jax.random.split(streams[6], N_TY * N_TX)
    slot_order = jax.vmap(lambda item: jax.random.permutation(item, COLS))(slot_keys).reshape(N_TY, N_TX, COLS).astype(jnp.int32)
    inclusive = jnp.cumsum(counts, axis=2).astype(jnp.int32)
    exclusive = inclusive - counts
    position = jnp.arange(COLS, dtype=jnp.int32)
    partner = jax.vmap(jax.vmap(lambda edges: jnp.searchsorted(edges, position, side='right')))(inclusive).astype(jnp.int32)
    group_idx = jnp.arange(N_TY, dtype=jnp.int32)[:, None, None]
    area_idx = jnp.arange(N_TX, dtype=jnp.int32)[None, :, None]
    offset = position[None, None, :] - exclusive[group_idx, area_idx, partner]
    vol_start = exclusive[group_idx, partner, area_idx]
    slot = slot_order[group_idx, partner, vol_start + offset]
    vol_index = partner * COLS + slot
    cell_index = area_idx * COLS + cell_order
    group_full = jnp.broadcast_to(group_idx, vol_index.shape)
    cell_of_vol = jnp.zeros((N_TY, cells), jnp.int32).at[group_full, vol_index].set(cell_index)
    rows = jnp.arange(N_TY, dtype=jnp.int32)[:, None]
    vol_levels = bathymetry[rows, cell_of_vol]
    own_value = jnp.where(partner == area_idx, slot, -1).astype(jnp.int32)
    own_local = jnp.full((N_TY, N_TX, COLS), -1, jnp.int32).at[group_full, jnp.broadcast_to(area_idx, vol_index.shape), cell_order].set(own_value)
    slot_idx = jnp.arange(CAP, dtype=jnp.int32)[None, None, None, :]
    where_at = jnp.minimum(exclusive[:, :, :, None] + slot_idx, COLS - 1)
    valid = (slot_idx < counts[:, :, :, None]) & (index[None, :, None, None] != index[None, None, :, None])
    group_four = jnp.arange(N_TY, dtype=jnp.int32)[:, None, None, None]
    first_four = jnp.arange(N_TX, dtype=jnp.int32)[None, :, None, None]
    sends = jnp.where(valid, slot_order[group_four, first_four, where_at], -1).astype(jnp.int32)
    receives = jnp.where(valid, cell_order[group_four, first_four, where_at], -1).astype(jnp.int32)
    return (bathymetry, vol_levels, own_local, sends, receives)


def to_area(values):
    shaped = values.reshape(N_TY, NXG, AY)
    return jnp.transpose(shaped, (1, 0, 2)).reshape(NXG, NYG)


def draw_levels(key, part):
    return layout(key)[1]


def draw_surface_levels(key, part):
    return to_area(layout(key)[0])


def draw_own_slot(key, part):
    return to_area(layout(key)[2])


def draw_send_list(key, part):
    return layout(key)[3]


def draw_receive_cell(key, part):
    return layout(key)[4]


def block_levels(key, extent, cuts, smallest, high):
    loudness, own = 1.0, jax.random.fold_in(key, 6)
    for dim, shards_of in cuts:
        steps = jnp.exp(jax.random.uniform(jax.random.fold_in(own, dim), (shards_of,), jnp.float32, smallest / len(cuts), high / len(cuts)))
        loudness = loudness * jnp.repeat(steps, extent[dim] // shards_of).reshape([-1 if axis == dim else 1 for axis in range(len(extent))])
    return loudness


def scatter_about(stream_key, shape, deviation, most, pieces=(), kind=jnp.bfloat16):
    array = jax.random.normal(stream_key, shape, jnp.float32) * deviation
    if len(pieces) > 0:
        array = block_levels(stream_key, shape, pieces, -0.22, 0.18) * array
    return jnp.clip(array, min=-most, max=most).astype(kind)


def setup_inputs(seed: int = 0) -> dict:
    splits = jax.random.split(jax.random.key(seed), 12)
    return {
        "velocity": scatter_about(splits[0], (2, LEV, N_TY, VCOLS), 1.0, 6.0, ((2, 4), (3, 8))),
        "tracers": scatter_about(splits[1], (2, LEV, N_TY, VCOLS), 1.0, 6.0, ((2, 4), (3, 8))),
        "surface_forcing": scatter_about(splits[2], (4, N_TY, VCOLS), 1.0, 6.0, ((1, 4), (2, 8)), jnp.float32),
        "thickness": jnp.clip(jnp.exp(jax.random.uniform(splits[3], (LEV,), jnp.float32, math.log(0.5), math.log(2.0))), 0.5, 2.0),
        "levels": draw_levels(jax.random.fold_in(splits[11], 71), 0),
        "surface_levels": draw_surface_levels(jax.random.fold_in(splits[11], 71), 0),
        "height": scatter_about(splits[6], (NXG, NYG), 1.0, 6.0, ((0, 8), (1, 4)), jnp.float32),
        "transport": scatter_about(splits[7], (2, NXG, NYG), 2.0, 12.0, ((1, 8), (2, 4)), jnp.float32),
        "send_list": draw_send_list(jax.random.fold_in(splits[11], 71), 0),
        "receive_cell": draw_receive_cell(jax.random.fold_in(splits[11], 71), 0),
        "own_slot": draw_own_slot(jax.random.fold_in(splits[11], 71), 0),
    }


time_step = 0.5
coriolis = 0.3
mixing = 200.0
height_rate = 0.25
transport_rate = 0.9
depth_floor = 1.0


def vertical_mix(rhs, wet_levels, thick):
    conduct = mixing * wet_levels[:-1] * wet_levels[1:] * (2.0 / (thick[:-1] + thick[1:]))[:, None]
    zero_row = jnp.zeros_like(wet_levels[:1])
    below = jnp.concatenate([conduct, zero_row], axis=0)
    above = jnp.concatenate([zero_row, conduct], axis=0)
    lower = -time_step * above / thick[:, None]
    upper = -time_step * below / thick[:, None]
    middle = 1.0 - lower - upper

    def sweep(carry, item):
        ratio, value = carry
        low, mid, upp, row = item
        denom = mid - low * ratio
        new_ratio = upp / denom
        new_value = (row - low[None] * value) / denom[None]
        return (new_ratio, new_value), (new_ratio, new_value)

    start = (jnp.zeros(rhs.shape[2:], jnp.float32), jnp.zeros(rhs.shape[1:], jnp.float32))
    ignored, stacks = lax.scan(sweep, start, (lower, middle, upper, rhs))
    ratios, values = stacks

    def backward(carry, item):
        ratio, value = item
        result = value - ratio[None] * carry
        return result, result

    ignored, solved = lax.scan(backward, jnp.zeros(rhs.shape[1:], jnp.float32), (ratios, values), reverse=True)
    return solved


def column_tendency(fields, forcing, lev_count, thick):
    wet_levels = (jnp.arange(LEV)[:, None] < lev_count[None, :]).astype(jnp.float32)
    surface_row = ((jnp.arange(LEV) == 0).astype(jnp.float32) / thick[0])[:, None, None]
    rotated = jnp.stack([coriolis * fields[:, 1], -coriolis * fields[:, 0]], axis=1)
    flow_tend = (rotated + surface_row * forcing[None, :2]) * wet_levels[:, None]
    tracer_tend = surface_row * forcing[None, 2:] * wet_levels[:, None]
    forcing_sum = jnp.sum(thick[:, None, None] * flow_tend, axis=0)
    return wet_levels, jnp.concatenate([flow_tend, tracer_tend], axis=1), forcing_sum


def column_terms(fields, forcing, lev_count, thick):
    wet_levels, tendency, forcing_sum = column_tendency(fields, forcing, lev_count, thick)
    rhs = wet_levels[:, None] * (fields + time_step * tendency)
    mixed = vertical_mix(rhs, wet_levels, thick)
    column_depth = jnp.sum(thick[:, None] * wet_levels, axis=0)
    return mixed, forcing_sum, column_depth, wet_levels


def correct(mixed, slot_flow, column_depth, wet_levels, thick):
    depth_sum = jnp.sum(thick[:, None, None] * mixed[:, :2], axis=0)
    shift = (slot_flow - depth_sum) / jnp.maximum(column_depth, depth_floor)[None]
    flow = wet_levels[:, None] * (mixed[:, :2] + shift[None])
    return jnp.concatenate([flow, mixed[:, 2:]], axis=1)


def substep(surface, east_flow, north_flow, force_east, force_north, depth):
    face_east = jnp.minimum(depth[:-1, :], depth[1:, :])
    face_north = jnp.minimum(depth[:, :-1], depth[:, 1:])
    spread = east_flow[1:, 1:] - east_flow[:-1, 1:] + north_flow[1:, 1:] - north_flow[1:, :-1]
    raised = surface[1:, 1:] - height_rate * spread
    slope_east = raised[1:, :-1] - raised[:-1, :-1]
    slope_north = raised[:-1, 1:] - raised[:-1, :-1]
    depth_east = face_east[1:, 1:-1]
    depth_north = face_north[1:-1, 1:]
    rate = transport_rate / LEV
    new_east = jnp.where(depth_east > 0, east_flow[1:-1, 1:-1] + rate * (force_east[1:-1, 1:-1] - depth_east * slope_east), 0.0)
    new_north = jnp.where(depth_north > 0, north_flow[1:-1, 1:-1] + rate * (force_north[1:-1, 1:-1] - depth_north * slope_north), 0.0)
    return raised[:-1, :-1], new_east, new_north


def group_to_area(values):
    leading = values.shape[:-2]
    shaped = values.reshape(leading + (N_TY, NXG, AY))
    shaped = jnp.swapaxes(shaped, -3, -2)
    return shaped.reshape(leading + (NXG, NYG))


def area_to_group(values):
    leading = values.shape[:-2]
    shaped = values.reshape(leading + (NXG, N_TY, AY))
    shaped = jnp.swapaxes(shaped, -3, -2)
    return shaped.reshape(leading + (N_TY, N_TX * COLS))


def layout_maps(send_list, receive_cell, own_slot):
    cells = N_TX * COLS
    own_group = area_to_group(own_slot)
    cell_ids = jnp.arange(cells, dtype=jnp.int32)
    owner = cell_ids // COLS
    own_vol = jnp.where(own_group >= 0, owner[None] * COLS + own_group, cells).astype(jnp.int32)
    sender = jnp.arange(N_TX, dtype=jnp.int32)[None, :, None, None]
    target = jnp.arange(N_TX, dtype=jnp.int32)[None, None, :, None]
    turned = jnp.swapaxes(receive_cell, 1, 2)
    valid = send_list >= 0
    cell_index = jnp.where(valid, target * COLS + turned, cells).astype(jnp.int32)
    vol_index = (sender * COLS + send_list).astype(jnp.int32)
    group_rows = jnp.broadcast_to(jnp.arange(N_TY, dtype=jnp.int32)[:, None, None, None], cell_index.shape)
    vol_of_cell = jnp.concatenate([own_vol, jnp.full((N_TY, 1), cells, jnp.int32)], axis=1)
    vol_of_cell = vol_of_cell.at[group_rows, cell_index].set(vol_index)[:, :cells]
    rows = jnp.broadcast_to(jnp.arange(N_TY, dtype=jnp.int32)[:, None], (N_TY, cells))
    cell_of_vol = jnp.zeros((N_TY, cells), jnp.int32).at[rows, vol_of_cell].set(jnp.broadcast_to(cell_ids[None], (N_TY, cells)))
    return vol_of_cell, cell_of_vol, rows


def reference(velocity, tracers, surface_forcing, thickness, levels, surface_levels, height, transport, send_list, receive_cell, own_slot):
    vol_of_cell, cell_of_vol, rows = layout_maps(send_list, receive_cell, own_slot)
    table = jnp.concatenate([jnp.zeros((1,), jnp.float32), jnp.cumsum(thickness)])
    surface_depth = table[surface_levels]
    fields = jnp.concatenate([velocity, tracers], axis=0).astype(jnp.float32)
    fields = jnp.transpose(fields, (2, 1, 0, 3))
    forcing_group = jnp.transpose(surface_forcing, (1, 0, 2))
    surface = height
    east_flow = transport[0]
    north_flow = transport[1]
    depth_pad = jnp.pad(surface_depth, 1)
    for ocean_step in range(STEPS):
        def force_pass(item):
            column_fields, column_forcing, lev_count = item
            return column_tendency(column_fields, column_forcing, lev_count, thickness)[2]

        forcing_sum = lax.map(force_pass, (fields, forcing_group, levels))
        forcing_sum = jnp.swapaxes(forcing_sum, 0, 1)
        force = group_to_area(forcing_sum[:, rows, vol_of_cell])
        force_east = jnp.pad(force[0], 1)
        force_north = jnp.pad(force[1], 1)
        total_east = jnp.zeros_like(east_flow)
        total_north = jnp.zeros_like(north_flow)
        for sub in range(NSUB):
            surface, east_flow, north_flow = substep(jnp.pad(surface, 1), jnp.pad(east_flow, 1), jnp.pad(north_flow, 1), force_east, force_north, depth_pad)
            total_east = total_east + east_flow
            total_north = total_north + north_flow
        mean_flow = jnp.stack([total_east, total_north]) / NSUB
        mean_group = area_to_group(mean_flow)
        slot_flow = jnp.swapaxes(mean_group[:, rows, cell_of_vol], 0, 1)

        def column_pass(item):
            column_fields, column_forcing, lev_count, column_flow = item
            mixed, ignored, column_depth, wet_levels = column_terms(column_fields, column_forcing, lev_count, thickness)
            return correct(mixed, column_flow, column_depth, wet_levels, thickness)

        fields = lax.map(column_pass, (fields, forcing_group, levels, slot_flow))
    result = jnp.transpose(fields, (2, 1, 0, 3))
    new_velocity = result[:2].astype(jnp.bfloat16)
    new_tracers = result[2:].astype(jnp.bfloat16)
    return new_velocity, new_tracers, surface, jnp.stack([east_flow, north_flow])
```

```python
import functools

import jax
import jax.numpy as jnp
from jax import lax
from jax.experimental import pallas as pl
from jax.experimental.pallas import tpu as pltpu
from jax.sharding import PartitionSpec as P

LEV = 60
NSUB = 16
STEPS = 2

time_step = 0.5
coriolis = 0.3
mixing = 200.0
height_rate = 0.25
transport_rate = 0.9
depth_floor = 1.0

LANES = 128
HALO = NSUB * STEPS
OFFSETS = [(dx, dy) for dx in (-2, -1, 0, 1, 2) for dy in (-1, 0, 1) if (dx, dy) != (0, 0)]


def slot_of(dx, dy):
    return (dx + 2) * 3 + dy + 1


def split3(x):
    high = x.astype(jnp.bfloat16)
    rest = x - high.astype(jnp.float32)
    mid = rest.astype(jnp.bfloat16)
    low = (rest - mid.astype(jnp.float32)).astype(jnp.bfloat16)
    return high, mid, low


def one_hot(lane_idx):
    shape = (LANES, lane_idx.shape[1])
    hit = lax.broadcasted_iota(jnp.int32, shape, 0) == lane_idx
    return jnp.where(hit, 1.0, 0.0).astype(jnp.bfloat16)


def pack(values, count, row_idx, hot):
    rows = values.shape[0] // count
    entries = hot.shape[1]
    got = None
    for part in split3(values):
        term = jnp.dot(part, hot, preferred_element_type=jnp.float32)
        got = term if got is None else got + term
    got = got.reshape(count, rows, entries)
    hit = lax.broadcasted_iota(jnp.int32, (1, rows, entries), 1) == row_idx[None]
    return jnp.sum(jnp.where(hit, got, 0.0), axis=1)


def unpack(entries, rows, row_idx, hot):
    count, size = entries.shape
    hit = lax.broadcasted_iota(jnp.int32, (1, rows, size), 1) == row_idx[None]
    total = None
    for part in split3(entries):
        spread = jnp.where(hit, part.astype(jnp.float32)[:, None, :], 0.0)
        spread = spread.reshape(count * rows, size).astype(jnp.bfloat16)
        term = lax.dot_general(
            spread, hot, (((1,), (1,)), ((), ())), preferred_element_type=jnp.float32
        )
        total = term if total is None else total + term
    return total


def kernel(
    n_tx,
    n_ty,
    coef,
    vel,
    trc,
    forcing,
    levels,
    area_levels,
    area,
    slot_idx,
    cell_idx,
    out_vel,
    out_trc,
    out_area,
    low_s,
    inv_s,
    ratio_s,
    val,
    a2a_out,
    a2a_in,
    pair_out,
    right_out,
    left_out,
    pair_in,
    side_in,
    win,
    a2a_send,
    a2a_recv,
    halo_send,
    halo_recv,
):
    tx = lax.axis_index("tx")
    ty = lax.axis_index("ty")
    rows = area.shape[1]
    cols = LANES - 2 * HALO
    brows = forcing.shape[1]
    remote = n_tx * LANES
    local = rows * cols

    def present(dx, dy):
        return (tx + dx >= 0) & (tx + dx < n_tx) & (ty + dy >= 0) & (ty + dy < n_ty)

    barrier = pltpu.get_barrier_semaphore()

    def greet(step, carry):
        pl.semaphore_signal(
            barrier,
            inc=1,
            device_id={"tx": lax.rem(tx + step, n_tx), "ty": ty},
            device_id_type=pl.DeviceIdType.MESH,
        )
        return carry

    a2a_in[...] = jnp.zeros_like(a2a_in)
    pair_in[...] = jnp.zeros_like(pair_in)
    side_in[...] = jnp.zeros_like(side_in)

    lax.fori_loop(1, n_tx, greet, 0)
    for dx, dy in OFFSETS:
        if dy != 0:

            @pl.when(present(dx, dy))
            def _():
                pl.semaphore_signal(
                    barrier,
                    inc=1,
                    device_id={"tx": tx + dx, "ty": ty + dy},
                    device_id_type=pl.DeviceIdType.MESH,
                )

    lev = levels[...]
    wet0 = lev > 0

    def add_level(k, carry):
        su, sv, depth, area_depth = carry
        t = coef[0, k]
        wet = jnp.where(lev > k, t, 0.0)
        su = su + wet * vel[0, k].astype(jnp.float32)
        sv = sv + wet * vel[1, k].astype(jnp.float32)
        area_depth = area_depth + jnp.where(area_levels[...] > k, t, 0.0)
        return su, sv, depth + wet, area_depth

    zero = jnp.zeros((brows, LANES), jnp.float32)
    sum_u, sum_v, depth, area_depth = lax.fori_loop(
        0, LEV, add_level, (zero, zero, zero, jnp.zeros((rows, LANES), jnp.float32))
    )
    wind_x = jnp.where(wet0, forcing[0], 0.0)
    wind_y = jnp.where(wet0, forcing[1], 0.0)
    payload = jnp.concatenate([sum_u, sum_v, wind_x, wind_y], axis=0)

    def slots(start, size):
        idx = slot_idx[:, start : start + size]
        return idx >> 7, one_hot(idx & (LANES - 1))

    def cells(start, size):
        idx = cell_idx[:, start : start + size]
        return lax.div(idx + cols, cols) - 1, one_hot(lax.rem(idx + cols, cols))

    chunk = min(1024, remote)
    per_chunk = chunk // LANES
    chunks = range(0, remote, chunk)

    def exchange_copy(stage, peer, mine):
        return pltpu.make_async_remote_copy(
            src_ref=a2a_out.at[stage, peer],
            dst_ref=a2a_in.at[stage, mine],
            send_sem=a2a_send.at[stage, peer],
            recv_sem=a2a_recv.at[stage, mine],
            device_id={"tx": peer, "ty": ty},
            device_id_type=pl.DeviceIdType.MESH,
        )

    def start_exchange(stage):
        def go(step, carry):
            exchange_copy(stage, lax.rem(tx + step, n_tx), tx).start()
            return carry

        lax.fori_loop(1, n_tx, go, 0)

    def finish_exchange(stage):
        def go(step, carry):
            exchange_copy(stage, lax.rem(tx + step, n_tx), tx).wait_send()
            source = lax.rem(tx + step, n_tx)
            exchange_copy(stage, source, source).wait_recv()
            return carry

        lax.fori_loop(1, n_tx, go, 0)

    def stage_out(stage, first, packed):
        for block in range(per_chunk):
            a2a_out[stage, first // LANES + block] = packed[:, block * LANES : (block + 1) * LANES]

    def stage_in(stage, first):
        return jnp.concatenate(
            [a2a_in[stage, first // LANES + block] for block in range(per_chunk)], axis=1
        )

    for first in chunks:
        row_idx, hot = slots(first, chunk)
        stage_out(0, first, pack(payload, 4, row_idx, hot))

    greeted = jnp.int32(n_tx - 1)
    for dx, dy in OFFSETS:
        if dy != 0:
            greeted = greeted + jnp.where(present(dx, dy), 1, 0)
    pl.semaphore_wait(barrier, greeted)
    start_exchange(0)

    lane = lax.broadcasted_iota(jnp.int32, (rows, LANES), 1)

    def halo_copy(stage, dx, dy):
        there = slot_of(-dx, -dy)
        if dy == 0:
            src, dst = pair_out.at[stage], pair_in.at[stage, 2 - dx]
        else:
            src = (right_out if dy > 0 else left_out).at[stage]
            dst = side_in.at[stage, 2 - dx, 0 if dy > 0 else 1]
        return pltpu.make_async_remote_copy(
            src_ref=src,
            dst_ref=dst,
            send_sem=halo_send.at[stage, slot_of(dx, dy)],
            recv_sem=halo_recv.at[stage, there],
            device_id={"tx": tx + dx, "ty": ty + dy},
            device_id_type=pl.DeviceIdType.MESH,
        )

    def start_halo(stage, tiles):
        for half in range(2):
            pair_out[stage, half] = jnp.where(
                lane < cols, tiles[2 * half], pltpu.roll(tiles[2 * half + 1], cols, 1)
            )
        right = jnp.zeros((rows, LANES), jnp.float32)
        left = jnp.zeros((rows, LANES), jnp.float32)
        for f in range(4):
            here = (lane >= HALO * f) & (lane < HALO * (f + 1))
            shift = (HALO * f - (cols - HALO)) % LANES
            right = jnp.where(here, pltpu.roll(tiles[f], shift, 1) if shift else tiles[f], right)
            shift = HALO * f
            left = jnp.where(here, pltpu.roll(tiles[f], shift, 1) if shift else tiles[f], left)
        right_out[stage] = right
        left_out[stage] = left
        for dx, dy in OFFSETS:

            @pl.when(present(dx, dy))
            def _():
                halo_copy(stage, dx, dy).start()

    def roll_lanes(x, shift):
        shift = shift % LANES
        return pltpu.roll(x, shift, 1) if shift else x

    def finish_halo(stage, tiles):
        for dx, dy in OFFSETS:

            @pl.when(present(dx, dy))
            def _():
                halo_copy(stage, dx, dy).wait_send()
                halo_copy(stage, -dx, -dy).wait_recv()

        for dx in (-2, -1, 0, 1, 2):
            from_left = side_in[stage, dx + 2, 0]
            from_right = side_in[stage, dx + 2, 1]
            for f in range(4):
                if dx == 0:
                    middle = roll_lanes(tiles[f], HALO)
                else:
                    pair = pair_in[stage, dx + 2, f // 2]
                    middle = roll_lanes(pair, HALO if f % 2 == 0 else HALO - cols)
                block = jnp.where(
                    lane < HALO,
                    roll_lanes(from_left, -HALO * f),
                    jnp.where(
                        lane >= HALO + cols,
                        roll_lanes(from_right, HALO + cols - HALO * f),
                        middle,
                    ),
                )
                win[stage * 4 + f, (dx + 2) * rows : (dx + 3) * rows, :] = block

    state_tiles = [area[0], area[1], area[2], area_depth]
    start_halo(0, state_tiles)

    inv_top = coef[3, 0]
    heat = jnp.where(wet0, time_step * inv_top * forcing[2], 0.0)
    salt = jnp.where(wet0, time_step * inv_top * forcing[3], 0.0)
    push_x = time_step * inv_top * wind_x
    push_y = time_step * inv_top * wind_y
    tilt = time_step * coriolis

    def top_term(k, x):
        return jnp.where(k == 0, x, 0.0)

    def first_forward(k, carry):
        ratio, u, v, a, b = carry
        wet = lev > k
        low = jnp.where(wet, -coef[1, k], 0.0)
        upp = jnp.where(lev > k + 1, -coef[2, k], 0.0)
        inv = 1.0 / (1.0 - low - upp - low * ratio)
        ratio = upp * inv
        low_inv = low * inv
        ratio_s[k] = ratio
        low_s[k] = low_inv
        inv_s[k] = inv
        uu = vel[0, k].astype(jnp.float32)
        vv = vel[1, k].astype(jnp.float32)
        wet_inv = jnp.where(wet, inv, 0.0)
        u = (uu + tilt * vv + top_term(k, push_x)) * wet_inv - low_inv * u
        v = (vv - tilt * uu + top_term(k, push_y)) * wet_inv - low_inv * v
        a = (trc[0, k].astype(jnp.float32) + top_term(k, heat)) * wet_inv - low_inv * a
        b = (trc[1, k].astype(jnp.float32) + top_term(k, salt)) * wet_inv - low_inv * b
        val[0, k] = u
        val[1, k] = v
        val[2, k] = a
        val[3, k] = b
        return ratio, u, v, a, b

    lax.fori_loop(0, LEV, first_forward, (zero, zero, zero, zero, zero))

    def gather_area():
        total = None
        for first in chunks:
            row_idx, hot = cells(first, chunk)
            term = unpack(stage_in(0, first), rows, row_idx, hot)
            total = term if total is None else total + term
        return total

    own_row, own_hot = slots(remote, local)
    own_vals = pack(payload, 4, own_row, own_hot)
    cell_row, cell_hot = cells(remote, local)
    own_area = unpack(own_vals, rows, cell_row, cell_hot)
    finish_exchange(0)
    tile = own_area + gather_area()
    sum_tiles = [tile[f * rows : (f + 1) * rows] for f in range(4)]
    start_halo(1, sum_tiles)

    def first_backward(step, carry):
        k = LEV - 1 - step
        u, v, a, b, du, dv = carry
        ratio = ratio_s[k]
        t = coef[0, k]
        u = val[0, k] - ratio * u
        v = val[1, k] - ratio * v
        a = val[2, k] - ratio * a
        b = val[3, k] - ratio * b
        val[0, k] = u
        val[1, k] = v
        val[2, k] = a
        val[3, k] = b
        return u, v, a, b, du + t * u, dv + t * v

    mixed = lax.fori_loop(0, LEV, first_backward, (zero,) * 6)
    first_du, first_dv = mixed[4], mixed[5]

    def second_forward(k, carry):
        u, v, a, b = carry
        low_inv = low_s[k]
        wet_inv = jnp.where(lev > k, inv_s[k], 0.0)
        uu = val[0, k]
        vv = val[1, k]
        u = (uu + tilt * vv + top_term(k, push_x)) * wet_inv - low_inv * u
        v = (vv - tilt * uu + top_term(k, push_y)) * wet_inv - low_inv * v
        a = (val[2, k] + top_term(k, heat)) * wet_inv - low_inv * a
        b = (val[3, k] + top_term(k, salt)) * wet_inv - low_inv * b
        val[0, k] = u
        val[1, k] = v
        val[2, k] = a
        val[3, k] = b
        return u, v, a, b

    lax.fori_loop(0, LEV, second_forward, (zero,) * 4)

    def second_backward(step, carry):
        k = LEV - 1 - step
        u, v, a, b, du, dv = carry
        ratio = ratio_s[k]
        t = coef[0, k]
        u = val[0, k] - ratio * u
        v = val[1, k] - ratio * v
        a = val[2, k] - ratio * a
        b = val[3, k] - ratio * b
        val[0, k] = u
        val[1, k] = v
        out_trc[0, k] = a.astype(jnp.bfloat16)
        out_trc[1, k] = b.astype(jnp.bfloat16)
        return u, v, a, b, du + t * u, dv + t * v

    mixed = lax.fori_loop(0, LEV, second_backward, (zero,) * 6)
    second_du, second_dv = mixed[4], mixed[5]

    finish_halo(0, state_tiles)
    finish_halo(1, sum_tiles)
    wrows = 5 * rows
    depth_w = win[3]
    rate = transport_rate / LEV
    face_e = jnp.minimum(depth_w, pltpu.roll(depth_w, wrows - 1, 0))
    face_n = jnp.minimum(depth_w, pltpu.roll(depth_w, LANES - 1, 1))
    rate_e = rate * face_e
    rate_n = rate * face_n
    su, sv, wx, wy = win[4], win[5], win[6], win[7]
    state = (win[0], win[1], win[2])
    means = []
    filled = depth_w / jnp.maximum(depth_w, depth_floor)
    for ocean_step in range(STEPS):
        force_e = coriolis * sv + wx
        force_n = wy - coriolis * su
        push_e = rate * force_e
        push_n = rate * force_n

        def substep(counter, carry):
            h, e, n, te, tn = carry
            spread = e - pltpu.roll(e, 1, 0) + n - pltpu.roll(n, 1, 1)
            h = h - height_rate * spread
            slope_e = pltpu.roll(h, wrows - 1, 0) - h
            slope_n = pltpu.roll(h, LANES - 1, 1) - h
            e = jnp.where(rate_e > 0, e + (push_e - rate_e * slope_e), 0.0)
            n = jnp.where(rate_n > 0, n + (push_n - rate_n * slope_n), 0.0)
            return h, e, n, te + e, tn + n

        nothing = jnp.zeros((wrows, LANES), jnp.float32)
        h, e, n, te, tn = lax.fori_loop(0, NSUB, substep, state + (nothing, nothing))
        state = (h, e, n)
        mean_e = te / NSUB
        mean_n = tn / NSUB
        means += [mean_e, mean_n]
        if ocean_step + 1 < STEPS:
            du = su + time_step * force_e
            dv = sv + time_step * force_n
            su = du + (mean_e - du) * filled
            sv = dv + (mean_n - dv) * filled

    def centre(x):
        return roll_lanes(x[2 * rows : 3 * rows], -HALO)

    flow = jnp.concatenate([centre(x) for x in means], axis=0)
    for first in chunks:
        row_idx, hot = cells(first, chunk)
        stage_out(1, first, pack(flow, 4, row_idx, hot))
    start_exchange(1)
    for f in range(3):
        out_area[f] = centre(state[f])
    slot_flow = unpack(pack(flow, 4, cell_row, cell_hot), brows, own_row, own_hot)
    finish_exchange(1)
    for first in chunks:
        row_idx, hot = slots(first, chunk)
        slot_flow = slot_flow + unpack(stage_in(1, first), brows, row_idx, hot)

    floor = jnp.maximum(depth, depth_floor)
    shift_u = (slot_flow[0:brows] - first_du) / floor
    shift_v = (slot_flow[brows : 2 * brows] - first_dv) / floor
    carry_u = shift_u + tilt * shift_v
    carry_v = shift_v - tilt * shift_u
    last_u = carry_u + (slot_flow[2 * brows : 3 * brows] - second_du - depth * carry_u) / floor
    last_v = carry_v + (slot_flow[3 * brows :] - second_dv - depth * carry_v) / floor

    def finish(k, carry):
        wet = lev > k
        out_vel[0, k] = (val[0, k] + jnp.where(wet, last_u, 0.0)).astype(jnp.bfloat16)
        out_vel[1, k] = (val[1, k] + jnp.where(wet, last_v, 0.0)).astype(jnp.bfloat16)
        return carry

    lax.fori_loop(0, LEV, finish, 0)


def body(
    n_tx,
    n_ty,
    velocity,
    tracers,
    surface_forcing,
    thickness,
    levels,
    surface_levels,
    height,
    transport,
    send_list,
    receive_cell,
    own_slot,
):
    rows, cols = height.shape
    slots = levels.shape[1]
    brows = slots // LANES
    cap = send_list.shape[3]
    vel = velocity.reshape(2, LEV, brows, LANES)
    trc = tracers.reshape(2, LEV, brows, LANES)
    forcing = surface_forcing.reshape(4, brows, LANES)
    gap = (0.5 * 2.0 * mixing) / (thickness[:-1] + thickness[1:])
    none = jnp.zeros((1,), jnp.float32)
    coef = jnp.stack(
        [
            thickness,
            jnp.concatenate([none, gap]) / thickness,
            jnp.concatenate([gap, none]) / thickness,
            1.0 / thickness,
        ]
    )
    pad = ((0, 0), (0, 0), (0, LANES - cap))
    sends = jnp.pad(send_list[0], pad, constant_values=-1).reshape(1, -1)
    receives = jnp.pad(receive_cell[0], pad, constant_values=-1).reshape(1, -1)
    slot_idx = jnp.concatenate([sends, own_slot.reshape(1, -1)], axis=1)
    cell_idx = jnp.concatenate(
        [receives, lax.broadcasted_iota(jnp.int32, (1, rows * cols), 1)], axis=1
    )
    area = jnp.concatenate([height[None], transport], axis=0)
    area = jnp.pad(area, ((0, 0), (0, 0), (0, LANES - cols)))
    area_levels = jnp.pad(surface_levels, ((0, 0), (0, LANES - cols)))
    vmem = pl.BlockSpec(memory_space=pltpu.VMEM)
    smem = pl.BlockSpec(memory_space=pltpu.SMEM)
    f32 = jnp.float32
    column = pltpu.VMEM((LEV, brows, LANES), f32)
    new_vel, new_trc, new_area = pl.pallas_call(
        functools.partial(kernel, n_tx, n_ty),
        out_shape=(
            jax.ShapeDtypeStruct((2, LEV, brows, LANES), jnp.bfloat16),
            jax.ShapeDtypeStruct((2, LEV, brows, LANES), jnp.bfloat16),
            jax.ShapeDtypeStruct((3, rows, LANES), f32),
        ),
        in_specs=[smem] + [vmem] * 8,
        out_specs=(vmem, vmem, vmem),
        scratch_shapes=[
            column,
            column,
            column,
            pltpu.VMEM((4, LEV, brows, LANES), f32),
            pltpu.VMEM((2, n_tx, 4, LANES), f32),
            pltpu.VMEM((2, n_tx, 4, LANES), f32),
            pltpu.VMEM((2, 2, rows, LANES), f32),
            pltpu.VMEM((2, rows, LANES), f32),
            pltpu.VMEM((2, rows, LANES), f32),
            pltpu.VMEM((2, 5, 2, rows, LANES), f32),
            pltpu.VMEM((2, 5, 2, rows, LANES), f32),
            pltpu.VMEM((8, 5 * rows, LANES), f32),
            pltpu.SemaphoreType.DMA((2, n_tx)),
            pltpu.SemaphoreType.DMA((2, n_tx)),
            pltpu.SemaphoreType.DMA((2, 15)),
            pltpu.SemaphoreType.DMA((2, 15)),
        ],
        compiler_params=pltpu.CompilerParams(
            collective_id=0, has_side_effects=True, vmem_limit_bytes=48 * 1024 * 1024
        ),
        name="ocean",
    )(coef, vel, trc, forcing, levels.reshape(brows, LANES), area_levels, area, slot_idx, cell_idx)
    new_velocity = new_vel.reshape(2, LEV, 1, slots)
    new_tracers = new_trc.reshape(2, LEV, 1, slots)
    return (new_velocity, new_tracers, new_area[0, :, :cols], new_area[1:, :, :cols])


def solution(mesh):
    in_specs = (
        P(None, None, "ty", "tx"),
        P(None, None, "ty", "tx"),
        P(None, "ty", "tx"),
        P(),
        P("ty", "tx"),
        P("tx", "ty"),
        P("tx", "ty"),
        P(None, "tx", "ty"),
        P("ty", "tx", None, None),
        P("ty", "tx", None, None),
        P("tx", "ty"),
    )
    out_specs = (
        P(None, None, "ty", "tx"),
        P(None, None, "ty", "tx"),
        P("tx", "ty"),
        P(None, "tx", "ty"),
    )
    return jax.shard_map(
        functools.partial(body, mesh.shape["tx"], mesh.shape["ty"]),
        mesh=mesh,
        in_specs=in_specs,
        out_specs=out_specs,
        check_vma=False,
    )
```

```python
import functools

import jax
import jax.numpy as jnp
from jax import lax
from jax.experimental import pallas as pl
from jax.experimental.pallas import tpu as pltpu
from jax.sharding import PartitionSpec as P

LEV = 60
NSUB = 16
STEPS = 2

time_step = 0.5
coriolis = 0.3
mixing = 200.0
height_rate = 0.25
transport_rate = 0.9
depth_floor = 1.0

LANES = 128
HALO = NSUB * STEPS
OFFSETS = [(dx, dy) for dx in (-2, -1, 0, 1, 2) for dy in (-1, 0, 1) if (dx, dy) != (0, 0)]


def slot_of(dx, dy):
    return (dx + 2) * 3 + dy + 1


def split3(x):
    high = x.astype(jnp.bfloat16)
    rest = x - high.astype(jnp.float32)
    mid = rest.astype(jnp.bfloat16)
    low = (rest - mid.astype(jnp.float32)).astype(jnp.bfloat16)
    return high, mid, low


def one_hot(lane_idx):
    shape = (LANES, lane_idx.shape[1])
    hit = lax.broadcasted_iota(jnp.int32, shape, 0) == lane_idx
    return jnp.where(hit, 1.0, 0.0).astype(jnp.bfloat16)


def pack(values, count, row_idx, hot):
    rows = values.shape[0] // count
    entries = hot.shape[1]
    got = None
    for part in split3(values):
        term = jnp.dot(part, hot, preferred_element_type=jnp.float32)
        got = term if got is None else got + term
    got = got.reshape(count, rows, entries)
    hit = lax.broadcasted_iota(jnp.int32, (1, rows, entries), 1) == row_idx[None]
    return jnp.sum(jnp.where(hit, got, 0.0), axis=1)


def unpack(entries, rows, row_idx, hot):
    count, size = entries.shape
    hit = lax.broadcasted_iota(jnp.int32, (1, rows, size), 1) == row_idx[None]
    total = None
    for part in split3(entries):
        spread = jnp.where(hit, part.astype(jnp.float32)[:, None, :], 0.0)
        spread = spread.reshape(count * rows, size).astype(jnp.bfloat16)
        term = lax.dot_general(
            spread, hot, (((1,), (1,)), ((), ())), preferred_element_type=jnp.float32
        )
        total = term if total is None else total + term
    return total


def kernel(
    n_tx,
    n_ty,
    thick_hbm,
    vel_hbm,
    trc_hbm,
    forcing_hbm,
    levels_hbm,
    area_levels_hbm,
    height_hbm,
    transport_hbm,
    send_hbm,
    receive_hbm,
    own_hbm,
    out_vel,
    out_trc,
    out_height,
    out_transport,
    thick_in,
    vel_in,
    trc_in,
    forcing,
    levels,
    area_levels_in,
    height_in,
    transport_in,
    send_in,
    receive_in,
    own_in,
    in_sem,
    coef,
    vel,
    trc,
    low_s,
    inv_s,
    ratio_s,
    val,
    a2a_out,
    a2a_in,
    pair_out,
    right_out,
    left_out,
    pair_in,
    side_in,
    win,
    a2a_send,
    a2a_recv,
    halo_send,
    halo_recv,
):
    tx = lax.axis_index("tx")
    ty = lax.axis_index("ty")
    rows = height_in.shape[0]
    cols = LANES - 2 * HALO
    brows = forcing.shape[1]
    remote = n_tx * LANES
    local = rows * cols

    def present(dx, dy):
        return (tx + dx >= 0) & (tx + dx < n_tx) & (ty + dy >= 0) & (ty + dy < n_ty)

    def fetch(number, src, dst):
        copy = pltpu.make_async_copy(src, dst, in_sem.at[number])
        copy.start()
        return copy

    vel_copy = fetch(0, vel_hbm, vel_in)
    thick_copy = fetch(1, thick_hbm, thick_in)
    level_copy = fetch(2, levels_hbm, levels)
    area_level_copy = fetch(3, area_levels_hbm, area_levels_in)
    forcing_copy = fetch(4, forcing_hbm, forcing)
    send_copy = fetch(5, send_hbm, send_in)
    height_copy = fetch(6, height_hbm, height_in)
    transport_copy = fetch(7, transport_hbm, transport_in)
    trc_copy = fetch(8, trc_hbm, trc_in)
    receive_copy = fetch(9, receive_hbm, receive_in)
    own_copy = fetch(10, own_hbm, own_in)

    barrier = pltpu.get_barrier_semaphore()

    def greet(step, carry):
        pl.semaphore_signal(
            barrier,
            inc=1,
            device_id={"tx": lax.rem(tx + step, n_tx), "ty": ty},
            device_id_type=pl.DeviceIdType.MESH,
        )
        return carry

    a2a_in[...] = jnp.zeros_like(a2a_in)
    pair_in[...] = jnp.zeros_like(pair_in)
    side_in[...] = jnp.zeros_like(side_in)

    lax.fori_loop(1, n_tx, greet, 0)
    for dx, dy in OFFSETS:
        if dy != 0:

            @pl.when(present(dx, dy))
            def _():
                pl.semaphore_signal(
                    barrier,
                    inc=1,
                    device_id={"tx": tx + dx, "ty": ty + dy},
                    device_id_type=pl.DeviceIdType.MESH,
                )

    thick_copy.wait()
    size = coef.shape[1]
    row_at = lax.broadcasted_iota(jnp.int32, (size, LANES), 0)
    lane_at = lax.broadcasted_iota(jnp.int32, (size, LANES), 1)
    row = thick_in[...]
    row = jnp.concatenate([row, jnp.ones((1, LANES - LEV), jnp.float32)], axis=1)

    def along_rows(x):
        column = jnp.sum(jnp.where(row_at == lane_at, x, 0.0), axis=1, keepdims=True)
        return jnp.broadcast_to(column, (size, LANES))

    thick = along_rows(row)
    gap = jnp.where(
        lane_at[:1] < LEV - 1, mixing / (row + pltpu.roll(row, LANES - 1, 1)), 0.0
    )
    coef[0] = thick
    coef[1] = along_rows(pltpu.roll(gap, 1, 1)) / thick
    coef[2] = along_rows(gap) / thick

    def at_level(which, k):
        return jnp.broadcast_to(coef[which, pl.ds(k, 1), :], (brows, LANES))

    def pair(ref, k):
        first = pl.multiple_of(k * 2 * brows, 2 * brows)
        return (
            ref[pl.ds(first, brows, stride=2), :],
            ref[pl.ds(first + 1, brows, stride=2), :],
        )

    def put_pair(ref, k, one, two):
        first = pl.multiple_of(k * 2 * brows, 2 * brows)
        ref[pl.ds(first, brows, stride=2), :] = one
        ref[pl.ds(first + 1, brows, stride=2), :] = two

    def sweep(step, carry, unroll):
        def several(block, inner):
            for sub in range(unroll):
                inner = step(block * unroll + sub, inner)
            return inner

        return lax.fori_loop(0, LEV // unroll, several, carry)

    level_copy.wait()
    area_level_copy.wait()
    lev = levels[...]
    wet0 = lev > 0

    def widen(x):
        return jnp.concatenate([x, jnp.zeros((rows, LANES - cols), x.dtype)], axis=1)

    area_lev = widen(area_levels_in[...])
    vel_copy.wait()
    vel[...] = vel_in[...].astype(jnp.float32)

    def add_level(k, carry):
        su, sv, depth, area_depth = carry
        t = at_level(0, k)
        wet = jnp.where(lev > k, t, 0.0)
        uu, vv = pair(vel, k)
        su = su + wet * uu
        sv = sv + wet * vv
        t = jnp.broadcast_to(coef[0, pl.ds(k, 1), :], (rows, LANES))
        area_depth = area_depth + jnp.where(area_lev > k, t, 0.0)
        return su, sv, depth + wet, area_depth

    zero = jnp.zeros((brows, LANES), jnp.float32)
    sum_u, sum_v, depth, area_depth = sweep(
        add_level, (zero, zero, zero, jnp.zeros((rows, LANES), jnp.float32)), 6
    )
    forcing_copy.wait()
    wind_x = jnp.where(wet0, forcing[0], 0.0)
    wind_y = jnp.where(wet0, forcing[1], 0.0)
    payload = jnp.concatenate([sum_u, sum_v, wind_x, wind_y], axis=0)

    def by_lanes(x):
        return jnp.concatenate([x[r : r + 1] for r in range(x.shape[0])], axis=1)

    def slots(start, size):
        idx = by_lanes(send_in[start // LANES : (start + size) // LANES, :])
        return idx >> 7, one_hot(idx & (LANES - 1))

    def own_slots():
        halves = LANES // cols
        got = [own_in[pl.ds(h, rows // halves, stride=halves), :] for h in range(halves)]
        idx = by_lanes(jnp.concatenate(got, axis=1))
        return idx >> 7, one_hot(idx & (LANES - 1))

    def cell_parts(idx):
        return lax.div(idx + cols, cols) - 1, one_hot(lax.rem(idx + cols, cols))

    def cells(start, size):
        return cell_parts(by_lanes(receive_in[start // LANES : (start + size) // LANES, :]))

    chunk = min(1024, remote)
    per_chunk = chunk // LANES
    chunks = range(0, remote, chunk)

    def exchange_copy(stage, peer, mine):
        return pltpu.make_async_remote_copy(
            src_ref=a2a_out.at[stage, peer],
            dst_ref=a2a_in.at[stage, mine],
            send_sem=a2a_send.at[stage, peer],
            recv_sem=a2a_recv.at[stage, mine],
            device_id={"tx": peer, "ty": ty},
            device_id_type=pl.DeviceIdType.MESH,
        )

    def start_exchange(stage):
        def go(step, carry):
            exchange_copy(stage, lax.rem(tx + step, n_tx), tx).start()
            return carry

        lax.fori_loop(1, n_tx, go, 0)

    def finish_exchange(stage):
        def go(step, carry):
            exchange_copy(stage, lax.rem(tx + step, n_tx), tx).wait_send()
            source = lax.rem(tx + step, n_tx)
            exchange_copy(stage, source, source).wait_recv()
            return carry

        lax.fori_loop(1, n_tx, go, 0)

    def stage_out(stage, first, packed):
        for block in range(per_chunk):
            a2a_out[stage, first // LANES + block] = packed[:, block * LANES : (block + 1) * LANES]

    def stage_in(stage, first):
        return jnp.concatenate(
            [a2a_in[stage, first // LANES + block] for block in range(per_chunk)], axis=1
        )

    send_copy.wait()
    for first in chunks:
        row_idx, hot = slots(first, chunk)
        stage_out(0, first, pack(payload, 4, row_idx, hot))

    greeted = jnp.int32(n_tx - 1)
    for dx, dy in OFFSETS:
        if dy != 0:
            greeted = greeted + jnp.where(present(dx, dy), 1, 0)
    pl.semaphore_wait(barrier, greeted)
    start_exchange(0)

    lane = lax.broadcasted_iota(jnp.int32, (rows, LANES), 1)

    def halo_copy(stage, dx, dy):
        there = slot_of(-dx, -dy)
        if dy == 0:
            src, dst = pair_out.at[stage], pair_in.at[stage, 2 - dx]
        else:
            src = (right_out if dy > 0 else left_out).at[stage]
            dst = side_in.at[stage, 2 - dx, 0 if dy > 0 else 1]
        return pltpu.make_async_remote_copy(
            src_ref=src,
            dst_ref=dst,
            send_sem=halo_send.at[stage, slot_of(dx, dy)],
            recv_sem=halo_recv.at[stage, there],
            device_id={"tx": tx + dx, "ty": ty + dy},
            device_id_type=pl.DeviceIdType.MESH,
        )

    def start_halo(stage, tiles):
        for half in range(2):
            pair_out[stage, half] = jnp.where(
                lane < cols, tiles[2 * half], pltpu.roll(tiles[2 * half + 1], cols, 1)
            )
        right = jnp.zeros((rows, LANES), jnp.float32)
        left = jnp.zeros((rows, LANES), jnp.float32)
        for f in range(4):
            here = (lane >= HALO * f) & (lane < HALO * (f + 1))
            shift = (HALO * f - (cols - HALO)) % LANES
            right = jnp.where(here, pltpu.roll(tiles[f], shift, 1) if shift else tiles[f], right)
            shift = HALO * f
            left = jnp.where(here, pltpu.roll(tiles[f], shift, 1) if shift else tiles[f], left)
        right_out[stage] = right
        left_out[stage] = left
        for dx, dy in OFFSETS:

            @pl.when(present(dx, dy))
            def _():
                halo_copy(stage, dx, dy).start()

    def roll_lanes(x, shift):
        shift = shift % LANES
        return pltpu.roll(x, shift, 1) if shift else x

    def finish_halo(stage, tiles):
        for dx, dy in OFFSETS:

            @pl.when(present(dx, dy))
            def _():
                halo_copy(stage, dx, dy).wait_send()
                halo_copy(stage, -dx, -dy).wait_recv()

        for dx in (-2, -1, 0, 1, 2):
            from_left = side_in[stage, dx + 2, 0]
            from_right = side_in[stage, dx + 2, 1]
            for f in range(4):
                if dx == 0:
                    middle = roll_lanes(tiles[f], HALO)
                else:
                    pair = pair_in[stage, dx + 2, f // 2]
                    middle = roll_lanes(pair, HALO if f % 2 == 0 else HALO - cols)
                block = jnp.where(
                    lane < HALO,
                    roll_lanes(from_left, -HALO * f),
                    jnp.where(
                        lane >= HALO + cols,
                        roll_lanes(from_right, HALO + cols - HALO * f),
                        middle,
                    ),
                )
                win[stage * 4 + f, (dx + 2) * rows : (dx + 3) * rows, :] = block

    height_copy.wait()
    transport_copy.wait()
    state_tiles = [
        widen(height_in[...]),
        widen(transport_in[0]),
        widen(transport_in[1]),
        area_depth,
    ]
    start_halo(0, state_tiles)

    trc_copy.wait()
    trc[...] = trc_in[...].astype(jnp.float32)
    inv_top = 1.0 / at_level(0, 0)
    heat = jnp.where(wet0, time_step * inv_top * forcing[2], 0.0)
    salt = jnp.where(wet0, time_step * inv_top * forcing[3], 0.0)
    push_x = time_step * inv_top * wind_x
    push_y = time_step * inv_top * wind_y
    tilt = time_step * coriolis

    def top_term(k, x):
        return jnp.where(k == 0, x, 0.0)

    def first_forward(k, carry):
        ratio, u, v, a, b = carry
        wet = lev > k
        low = jnp.where(wet, -at_level(1, k), 0.0)
        upp = jnp.where(lev > k + 1, -at_level(2, k), 0.0)
        inv = 1.0 / (1.0 - low - upp - low * ratio)
        ratio = upp * inv
        low_inv = low * inv
        ratio_s[k] = ratio
        low_s[k] = low_inv
        inv_s[k] = inv
        uu, vv = pair(vel, k)
        aa, bb = pair(trc, k)
        wet_inv = jnp.where(wet, inv, 0.0)
        u = (uu + tilt * vv + top_term(k, push_x)) * wet_inv - low_inv * u
        v = (vv - tilt * uu + top_term(k, push_y)) * wet_inv - low_inv * v
        a = (aa + top_term(k, heat)) * wet_inv - low_inv * a
        b = (bb + top_term(k, salt)) * wet_inv - low_inv * b
        val[0, k] = u
        val[1, k] = v
        val[2, k] = a
        val[3, k] = b
        return ratio, u, v, a, b

    sweep(first_forward, (zero, zero, zero, zero, zero), 4)

    def gather_area():
        total = None
        for first in chunks:
            row_idx, hot = cells(first, chunk)
            term = unpack(stage_in(0, first), rows, row_idx, hot)
            total = term if total is None else total + term
        return total

    own_copy.wait()
    receive_copy.wait()
    own_row, own_hot = own_slots()
    own_vals = pack(payload, 4, own_row, own_hot)
    cell_row, cell_hot = cell_parts(lax.broadcasted_iota(jnp.int32, (1, local), 1))
    own_area = unpack(own_vals, rows, cell_row, cell_hot)
    finish_exchange(0)
    tile = own_area + gather_area()
    sum_tiles = [tile[f * rows : (f + 1) * rows] for f in range(4)]
    start_halo(1, sum_tiles)

    def first_backward(step, carry):
        k = LEV - 1 - step
        u, v, a, b, du, dv = carry
        ratio = ratio_s[k]
        t = at_level(0, k)
        u = val[0, k] - ratio * u
        v = val[1, k] - ratio * v
        a = val[2, k] - ratio * a
        b = val[3, k] - ratio * b
        val[0, k] = u
        val[1, k] = v
        val[2, k] = a
        val[3, k] = b
        return u, v, a, b, du + t * u, dv + t * v

    mixed = sweep(first_backward, (zero,) * 6, 6)
    first_du, first_dv = mixed[4], mixed[5]

    finish_halo(0, state_tiles)
    finish_halo(1, sum_tiles)
    wrows = 5 * rows
    depth_w = win[3]
    rate = transport_rate / LEV
    face_e = jnp.minimum(depth_w, pltpu.roll(depth_w, wrows - 1, 0))
    face_n = jnp.minimum(depth_w, pltpu.roll(depth_w, LANES - 1, 1))
    rate_e = rate * face_e
    rate_n = rate * face_n
    su, sv, wx, wy = win[4], win[5], win[6], win[7]
    state = (win[0], win[1], win[2])
    means = []
    filled = depth_w / jnp.maximum(depth_w, depth_floor)
    for ocean_step in range(STEPS):
        force_e = coriolis * sv + wx
        force_n = wy - coriolis * su
        push_e = rate * force_e
        push_n = rate * force_n

        def substep(counter, carry):
            h, e, n, te, tn = carry
            spread = e - pltpu.roll(e, 1, 0) + n - pltpu.roll(n, 1, 1)
            h = h - height_rate * spread
            slope_e = pltpu.roll(h, wrows - 1, 0) - h
            slope_n = pltpu.roll(h, LANES - 1, 1) - h
            e = jnp.where(rate_e > 0, e + (push_e - rate_e * slope_e), 0.0)
            n = jnp.where(rate_n > 0, n + (push_n - rate_n * slope_n), 0.0)
            return h, e, n, te + e, tn + n

        nothing = jnp.zeros((wrows, LANES), jnp.float32)
        h, e, n, te, tn = lax.fori_loop(0, NSUB, substep, state + (nothing, nothing))
        state = (h, e, n)
        mean_e = te / NSUB
        mean_n = tn / NSUB
        means += [mean_e, mean_n]
        if ocean_step + 1 < STEPS:
            du = su + time_step * force_e
            dv = sv + time_step * force_n
            su = du + (mean_e - du) * filled
            sv = dv + (mean_n - dv) * filled

    def centre(x):
        return roll_lanes(x[2 * rows : 3 * rows], -HALO)

    flow = jnp.concatenate([centre(x) for x in means], axis=0)
    for first in chunks:
        row_idx, hot = cells(first, chunk)
        stage_out(1, first, pack(flow, 4, row_idx, hot))
    start_exchange(1)
    def second_forward(k, carry):
        u, v, a, b = carry
        low_inv = low_s[k]
        wet_inv = jnp.where(lev > k, inv_s[k], 0.0)
        uu = val[0, k]
        vv = val[1, k]
        u = (uu + tilt * vv + top_term(k, push_x)) * wet_inv - low_inv * u
        v = (vv - tilt * uu + top_term(k, push_y)) * wet_inv - low_inv * v
        a = (val[2, k] + top_term(k, heat)) * wet_inv - low_inv * a
        b = (val[3, k] + top_term(k, salt)) * wet_inv - low_inv * b
        val[0, k] = u
        val[1, k] = v
        val[2, k] = a
        val[3, k] = b
        return u, v, a, b

    sweep(second_forward, (zero,) * 4, 6)

    def second_backward(step, carry):
        k = LEV - 1 - step
        u, v, a, b, du, dv = carry
        ratio = ratio_s[k]
        t = at_level(0, k)
        u = val[0, k] - ratio * u
        v = val[1, k] - ratio * v
        a = val[2, k] - ratio * a
        b = val[3, k] - ratio * b
        val[0, k] = u
        val[1, k] = v
        put_pair(trc, k, a, b)
        return u, v, a, b, du + t * u, dv + t * v

    mixed = sweep(second_backward, (zero,) * 6, 6)
    second_du, second_dv = mixed[4], mixed[5]

    out_trc[...] = trc[...].astype(jnp.bfloat16)
    out_height[...] = centre(state[0])[:, :cols]
    out_transport[0] = centre(state[1])[:, :cols]
    out_transport[1] = centre(state[2])[:, :cols]
    slot_flow = unpack(pack(flow, 4, cell_row, cell_hot), brows, own_row, own_hot)
    finish_exchange(1)
    for first in chunks:
        row_idx, hot = slots(first, chunk)
        slot_flow = slot_flow + unpack(stage_in(1, first), brows, row_idx, hot)

    floor = jnp.maximum(depth, depth_floor)
    shift_u = (slot_flow[0:brows] - first_du) / floor
    shift_v = (slot_flow[brows : 2 * brows] - first_dv) / floor
    carry_u = shift_u + tilt * shift_v
    carry_v = shift_v - tilt * shift_u
    last_u = carry_u + (slot_flow[2 * brows : 3 * brows] - second_du - depth * carry_u) / floor
    last_v = carry_v + (slot_flow[3 * brows :] - second_dv - depth * carry_v) / floor

    def finish(k, carry):
        wet = lev > k
        put_pair(
            vel,
            k,
            val[0, k] + jnp.where(wet, last_u, 0.0),
            val[1, k] + jnp.where(wet, last_v, 0.0),
        )
        return carry

    sweep(finish, 0, 6)
    out_vel[...] = vel[...].astype(jnp.bfloat16)


def deliver(*refs):
    count = (len(refs) - 1) // 2
    sems = refs[-1]
    copies = [
        pltpu.make_async_copy(refs[i], refs[count + i], sems.at[i]) for i in range(count)
    ]
    for copy in copies:
        copy.start()
    for copy in copies:
        copy.wait()


def flat(x, brows):
    x = x.reshape(2, LEV, brows, LANES)
    return jnp.transpose(x, (1, 2, 0, 3)).reshape(LEV * brows * 2, LANES)


def unflat(x, brows):
    x = x.reshape(LEV, brows, 2, LANES)
    return jnp.transpose(x, (2, 0, 1, 3)).reshape(2, LEV, 1, brows * LANES)


def body(
    n_tx,
    n_ty,
    velocity,
    tracers,
    surface_forcing,
    thickness,
    levels,
    surface_levels,
    height,
    transport,
    send_list,
    receive_cell,
    own_slot,
):
    rows, cols = height.shape
    slots = levels.shape[1]
    brows = slots // LANES
    cap = send_list.shape[3]
    forcing = surface_forcing.reshape(4, brows, LANES)
    pad = ((0, 0), (0, 0), (0, LANES - cap))
    sends, receives = send_list[0], receive_cell[0]
    if cap < LANES:
        sends = jnp.pad(sends, pad, constant_values=-1)
        receives = jnp.pad(receives, pad, constant_values=-1)
    operands = (
        thickness.reshape(1, LEV),
        flat(velocity, brows),
        flat(tracers, brows),
        forcing,
        levels.reshape(brows, LANES),
        surface_levels,
        height,
        transport,
        sends[0],
        receives[0],
        own_slot,
    )
    vmem = pl.BlockSpec(memory_space=pltpu.VMEM)
    hbm = pl.BlockSpec(memory_space=pltpu.HBM)
    f32 = jnp.float32
    column = pltpu.VMEM((LEV, brows, LANES), f32)
    whole = (LEV * brows * 2, LANES)
    results = (
        jax.ShapeDtypeStruct(whole, jnp.bfloat16),
        jax.ShapeDtypeStruct(whole, jnp.bfloat16),
        jax.ShapeDtypeStruct((rows, cols), f32),
        jax.ShapeDtypeStruct((2, rows, cols), f32),
    )
    got = pl.pallas_call(
        functools.partial(kernel, n_tx, n_ty),
        out_shape=results,
        in_specs=[hbm] * len(operands),
        out_specs=(vmem,) * 4,
        scratch_shapes=[pltpu.VMEM(x.shape, x.dtype) for x in operands]
        + [
            pltpu.SemaphoreType.DMA((len(operands),)),
            pltpu.VMEM((3, 64, LANES), f32),
            pltpu.VMEM(whole, f32),
            pltpu.VMEM(whole, f32),
            column,
            column,
            column,
            pltpu.VMEM((4, LEV, brows, LANES), f32),
            pltpu.VMEM((2, n_tx, 4, LANES), f32),
            pltpu.VMEM((2, n_tx, 4, LANES), f32),
            pltpu.VMEM((2, 2, rows, LANES), f32),
            pltpu.VMEM((2, rows, LANES), f32),
            pltpu.VMEM((2, rows, LANES), f32),
            pltpu.VMEM((2, 5, 2, rows, LANES), f32),
            pltpu.VMEM((2, 5, 2, rows, LANES), f32),
            pltpu.VMEM((8, 5 * rows, LANES), f32),
            pltpu.SemaphoreType.DMA((2, n_tx)),
            pltpu.SemaphoreType.DMA((2, n_tx)),
            pltpu.SemaphoreType.DMA((2, 15)),
            pltpu.SemaphoreType.DMA((2, 15)),
        ],
        compiler_params=pltpu.CompilerParams(
            collective_id=0, has_side_effects=True, vmem_limit_bytes=48 * 1024 * 1024
        ),
        name="ocean",
    )(*[pltpu.with_memory_space_constraint(x, pltpu.HBM) for x in operands])
    new_vel, new_trc, new_height, new_transport = pl.pallas_call(
        deliver,
        out_shape=results,
        in_specs=[vmem] * 4,
        out_specs=(hbm,) * 4,
        scratch_shapes=[pltpu.SemaphoreType.DMA((4,))],
        name="deliver",
    )(*[pltpu.with_memory_space_constraint(x, pltpu.VMEM) for x in got])
    return (unflat(new_vel, brows), unflat(new_trc, brows), new_height, new_transport)


def solution(mesh):
    in_specs = (
        P(None, None, "ty", "tx"),
        P(None, None, "ty", "tx"),
        P(None, "ty", "tx"),
        P(),
        P("ty", "tx"),
        P("tx", "ty"),
        P("tx", "ty"),
        P(None, "tx", "ty"),
        P("ty", "tx", None, None),
        P("ty", "tx", None, None),
        P("tx", "ty"),
    )
    out_specs = (
        P(None, None, "ty", "tx"),
        P(None, None, "ty", "tx"),
        P("tx", "ty"),
        P(None, "tx", "ty"),
    )
    return jax.shard_map(
        functools.partial(body, mesh.shape["tx"], mesh.shape["ty"]),
        mesh=mesh,
        in_specs=in_specs,
        out_specs=out_specs,
        check_vma=False,
    )
```

```python
import functools

import jax
import jax.numpy as jnp
from jax import lax
from jax.experimental import pallas as pl
from jax.experimental.pallas import tpu as pltpu
from jax.sharding import PartitionSpec as P

LEV = 60
NSUB = 16
STEPS = 2

time_step = 0.5
coriolis = 0.3
mixing = 200.0
height_rate = 0.25
transport_rate = 0.9
depth_floor = 1.0

LANES = 128
HALO = NSUB * STEPS
OFFSETS = [(dx, dy) for dx in (-2, -1, 0, 1, 2) for dy in (-1, 0, 1) if (dx, dy) != (0, 0)]


def slot_of(dx, dy):
    return (dx + 2) * 3 + dy + 1


def split3(x):
    high = x.astype(jnp.bfloat16)
    rest = x - high.astype(jnp.float32)
    mid = rest.astype(jnp.bfloat16)
    low = (rest - mid.astype(jnp.float32)).astype(jnp.bfloat16)
    return high, mid, low


def one_hot(lane_idx):
    shape = (LANES, lane_idx.shape[1])
    hit = lax.broadcasted_iota(jnp.int32, shape, 0) == lane_idx
    return jnp.where(hit, 1.0, 0.0).astype(jnp.bfloat16)


def pack(values, count, row_idx, hot):
    rows = values.shape[0] // count
    entries = hot.shape[1]
    got = None
    for part in split3(values):
        term = jnp.dot(part, hot, preferred_element_type=jnp.float32)
        got = term if got is None else got + term
    got = got.reshape(count, rows, entries)
    hit = lax.broadcasted_iota(jnp.int32, (1, rows, entries), 1) == row_idx[None]
    return jnp.sum(jnp.where(hit, got, 0.0), axis=1)


def unpack(entries, rows, row_idx, hot):
    count, size = entries.shape
    hit = lax.broadcasted_iota(jnp.int32, (1, rows, size), 1) == row_idx[None]
    total = None
    for part in split3(entries):
        spread = jnp.where(hit, part.astype(jnp.float32)[:, None, :], 0.0)
        spread = spread.reshape(count * rows, size).astype(jnp.bfloat16)
        term = lax.dot_general(
            spread, hot, (((1,), (1,)), ((), ())), preferred_element_type=jnp.float32
        )
        total = term if total is None else total + term
    return total


def kernel(
    n_tx,
    n_ty,
    thick_hbm,
    vel_hbm,
    trc_hbm,
    forcing_hbm,
    levels_hbm,
    area_levels_hbm,
    height_hbm,
    transport_hbm,
    send_hbm,
    receive_hbm,
    own_hbm,
    out_vel,
    out_trc,
    out_height,
    out_transport,
    thick_in,
    vel_in,
    trc_in,
    forcing,
    levels,
    area_levels_in,
    height_in,
    transport_in,
    send_in,
    receive_in,
    own_in,
    in_sem,
    coef,
    vel,
    trc,
    low_s,
    inv_s,
    ratio_s,
    val,
    a2a_out,
    a2a_in,
    pair_out,
    right_out,
    left_out,
    pair_in,
    side_in,
    win,
    a2a_send,
    a2a_recv,
    halo_send,
    halo_recv,
):
    tx = lax.axis_index("tx")
    ty = lax.axis_index("ty")
    rows = height_in.shape[0]
    cols = LANES - 2 * HALO
    brows = forcing.shape[1]
    remote = n_tx * LANES
    local = rows * cols

    def present(dx, dy):
        return (tx + dx >= 0) & (tx + dx < n_tx) & (ty + dy >= 0) & (ty + dy < n_ty)

    def fetch(number, src, dst):
        copy = pltpu.make_async_copy(src, dst, in_sem.at[number])
        copy.start()
        return copy

    vel_copy = fetch(0, vel_hbm, vel_in)
    thick_copy = fetch(1, thick_hbm, thick_in)
    level_copy = fetch(2, levels_hbm, levels)
    area_level_copy = fetch(3, area_levels_hbm, area_levels_in)
    forcing_copy = fetch(4, forcing_hbm, forcing)
    send_copy = fetch(5, send_hbm, send_in)
    height_copy = fetch(6, height_hbm, height_in)
    transport_copy = fetch(7, transport_hbm, transport_in)
    trc_copy = fetch(8, trc_hbm, trc_in)
    receive_copy = fetch(9, receive_hbm, receive_in)
    own_copy = fetch(10, own_hbm, own_in)

    barrier = pltpu.get_barrier_semaphore()

    def greet(step, carry):
        pl.semaphore_signal(
            barrier,
            inc=1,
            device_id={"tx": lax.rem(tx + step, n_tx), "ty": ty},
            device_id_type=pl.DeviceIdType.MESH,
        )
        return carry

    a2a_in[...] = jnp.zeros_like(a2a_in)
    pair_in[...] = jnp.zeros_like(pair_in)
    side_in[...] = jnp.zeros_like(side_in)

    lax.fori_loop(1, n_tx, greet, 0)
    for dx, dy in OFFSETS:
        if dy != 0:

            @pl.when(present(dx, dy))
            def _():
                pl.semaphore_signal(
                    barrier,
                    inc=1,
                    device_id={"tx": tx + dx, "ty": ty + dy},
                    device_id_type=pl.DeviceIdType.MESH,
                )

    thick_copy.wait()
    size = coef.shape[1]
    row_at = lax.broadcasted_iota(jnp.int32, (size, LANES), 0)
    lane_at = lax.broadcasted_iota(jnp.int32, (size, LANES), 1)
    row = thick_in[...]
    row = jnp.concatenate([row, jnp.ones((1, LANES - LEV), jnp.float32)], axis=1)

    def along_rows(x):
        column = jnp.sum(jnp.where(row_at == lane_at, x, 0.0), axis=1, keepdims=True)
        return jnp.broadcast_to(column, (size, LANES))

    thick = along_rows(row)
    gap = jnp.where(
        lane_at[:1] < LEV - 1, mixing / (row + pltpu.roll(row, LANES - 1, 1)), 0.0
    )
    coef[0] = thick
    coef[1] = along_rows(pltpu.roll(gap, 1, 1)) / thick
    coef[2] = along_rows(gap) / thick

    def at_level(which, k):
        return jnp.broadcast_to(coef[which, pl.ds(k, 1), :], (brows, LANES))

    def pair(ref, k):
        first = pl.multiple_of(k * 2 * brows, 2 * brows)
        return (
            ref[pl.ds(first, brows, stride=2), :],
            ref[pl.ds(first + 1, brows, stride=2), :],
        )

    def put_pair(ref, k, one, two):
        first = pl.multiple_of(k * 2 * brows, 2 * brows)
        ref[pl.ds(first, brows, stride=2), :] = one
        ref[pl.ds(first + 1, brows, stride=2), :] = two

    def sweep(step, carry, unroll):
        def several(block, inner):
            for sub in range(unroll):
                inner = step(block * unroll + sub, inner)
            return inner

        return lax.fori_loop(0, LEV // unroll, several, carry)

    level_copy.wait()
    area_level_copy.wait()
    lev = levels[...]
    wet0 = lev > 0

    def widen(x):
        return jnp.concatenate([x, jnp.zeros((rows, LANES - cols), x.dtype)], axis=1)

    area_lev = widen(area_levels_in[...])
    vel_copy.wait()
    vel[...] = vel_in[...].astype(jnp.float32)

    def add_level(k, carry):
        su, sv, depth, area_depth = carry
        t = at_level(0, k)
        wet = jnp.where(lev > k, t, 0.0)
        uu, vv = pair(vel, k)
        su = su + wet * uu
        sv = sv + wet * vv
        t = jnp.broadcast_to(coef[0, pl.ds(k, 1), :], (rows, LANES))
        area_depth = area_depth + jnp.where(area_lev > k, t, 0.0)
        return su, sv, depth + wet, area_depth

    zero = jnp.zeros((brows, LANES), jnp.float32)
    sum_u, sum_v, depth, area_depth = sweep(
        add_level, (zero, zero, zero, jnp.zeros((rows, LANES), jnp.float32)), 6
    )
    forcing_copy.wait()
    wind_x = jnp.where(wet0, forcing[0], 0.0)
    wind_y = jnp.where(wet0, forcing[1], 0.0)
    payload = jnp.concatenate([sum_u, sum_v, wind_x, wind_y], axis=0)

    def by_lanes(x):
        return jnp.concatenate([x[r : r + 1] for r in range(x.shape[0])], axis=1)

    def slots(start, size):
        idx = by_lanes(send_in[start // LANES : (start + size) // LANES, :])
        return idx >> 7, one_hot(idx & (LANES - 1))

    def own_slots():
        halves = LANES // cols
        got = [own_in[pl.ds(h, rows // halves, stride=halves), :] for h in range(halves)]
        idx = by_lanes(jnp.concatenate(got, axis=1))
        return idx >> 7, one_hot(idx & (LANES - 1))

    def cell_parts(idx):
        return lax.div(idx + cols, cols) - 1, one_hot(lax.rem(idx + cols, cols))

    def cells(start, size):
        return cell_parts(by_lanes(receive_in[start // LANES : (start + size) // LANES, :]))

    chunk = min(1024, remote)
    per_chunk = chunk // LANES
    chunks = range(0, remote, chunk)

    def exchange_copy(stage, peer, mine):
        return pltpu.make_async_remote_copy(
            src_ref=a2a_out.at[stage, peer],
            dst_ref=a2a_in.at[stage, mine],
            send_sem=a2a_send.at[stage, peer],
            recv_sem=a2a_recv.at[stage, mine],
            device_id={"tx": peer, "ty": ty},
            device_id_type=pl.DeviceIdType.MESH,
        )

    def start_exchange(stage):
        def go(step, carry):
            exchange_copy(stage, lax.rem(tx + step, n_tx), tx).start()
            return carry

        lax.fori_loop(1, n_tx, go, 0)

    def finish_exchange(stage):
        def go(step, carry):
            exchange_copy(stage, lax.rem(tx + step, n_tx), tx).wait_send()
            source = lax.rem(tx + step, n_tx)
            exchange_copy(stage, source, source).wait_recv()
            return carry

        lax.fori_loop(1, n_tx, go, 0)

    def stage_out(stage, first, packed):
        for block in range(per_chunk):
            a2a_out[stage, first // LANES + block] = packed[:, block * LANES : (block + 1) * LANES]

    def stage_in(stage, first):
        return jnp.concatenate(
            [a2a_in[stage, first // LANES + block] for block in range(per_chunk)], axis=1
        )

    send_copy.wait()
    slot_maps = [slots(first, chunk) for first in chunks]
    for first, (row_idx, hot) in zip(chunks, slot_maps):
        stage_out(0, first, pack(payload, 4, row_idx, hot))

    greeted = jnp.int32(n_tx - 1)
    for dx, dy in OFFSETS:
        if dy != 0:
            greeted = greeted + jnp.where(present(dx, dy), 1, 0)
    pl.semaphore_wait(barrier, greeted)
    start_exchange(0)

    lane = lax.broadcasted_iota(jnp.int32, (rows, LANES), 1)

    def halo_copy(stage, dx, dy):
        there = slot_of(-dx, -dy)
        if dy == 0:
            src, dst = pair_out.at[stage], pair_in.at[stage, 2 - dx]
        else:
            src = (right_out if dy > 0 else left_out).at[stage]
            dst = side_in.at[stage, 2 - dx, 0 if dy > 0 else 1]
        return pltpu.make_async_remote_copy(
            src_ref=src,
            dst_ref=dst,
            send_sem=halo_send.at[stage, slot_of(dx, dy)],
            recv_sem=halo_recv.at[stage, there],
            device_id={"tx": tx + dx, "ty": ty + dy},
            device_id_type=pl.DeviceIdType.MESH,
        )

    def start_halo(stage, tiles):
        for half in range(2):
            pair_out[stage, half] = jnp.where(
                lane < cols, tiles[2 * half], pltpu.roll(tiles[2 * half + 1], cols, 1)
            )
        right = jnp.zeros((rows, LANES), jnp.float32)
        left = jnp.zeros((rows, LANES), jnp.float32)
        for f in range(4):
            here = (lane >= HALO * f) & (lane < HALO * (f + 1))
            shift = (HALO * f - (cols - HALO)) % LANES
            right = jnp.where(here, pltpu.roll(tiles[f], shift, 1) if shift else tiles[f], right)
            shift = HALO * f
            left = jnp.where(here, pltpu.roll(tiles[f], shift, 1) if shift else tiles[f], left)
        right_out[stage] = right
        left_out[stage] = left
        for dx, dy in OFFSETS:

            @pl.when(present(dx, dy))
            def _():
                halo_copy(stage, dx, dy).start()

    def roll_lanes(x, shift):
        shift = shift % LANES
        return pltpu.roll(x, shift, 1) if shift else x

    def finish_halo(stage, tiles):
        for dx, dy in OFFSETS:

            @pl.when(present(dx, dy))
            def _():
                halo_copy(stage, dx, dy).wait_send()
                halo_copy(stage, -dx, -dy).wait_recv()

        for dx in (-2, -1, 0, 1, 2):
            from_left = side_in[stage, dx + 2, 0]
            from_right = side_in[stage, dx + 2, 1]
            for f in range(4):
                if dx == 0:
                    middle = roll_lanes(tiles[f], HALO)
                else:
                    pair = pair_in[stage, dx + 2, f // 2]
                    middle = roll_lanes(pair, HALO if f % 2 == 0 else HALO - cols)
                block = jnp.where(
                    lane < HALO,
                    roll_lanes(from_left, -HALO * f),
                    jnp.where(
                        lane >= HALO + cols,
                        roll_lanes(from_right, HALO + cols - HALO * f),
                        middle,
                    ),
                )
                win[stage * 4 + f, (dx + 2) * rows : (dx + 3) * rows, :] = block

    height_copy.wait()
    transport_copy.wait()
    state_tiles = [
        widen(height_in[...]),
        widen(transport_in[0]),
        widen(transport_in[1]),
        area_depth,
    ]
    start_halo(0, state_tiles)

    trc_copy.wait()
    trc[...] = trc_in[...].astype(jnp.float32)
    inv_top = 1.0 / at_level(0, 0)
    heat = jnp.where(wet0, time_step * inv_top * forcing[2], 0.0)
    salt = jnp.where(wet0, time_step * inv_top * forcing[3], 0.0)
    push_x = time_step * inv_top * wind_x
    push_y = time_step * inv_top * wind_y
    tilt = time_step * coriolis

    def top_term(k, x):
        return jnp.where(k == 0, x, 0.0)

    def first_forward(k, carry):
        ratio, u, v, a, b = carry
        wet = lev > k
        low = jnp.where(wet, -at_level(1, k), 0.0)
        upp = jnp.where(lev > k + 1, -at_level(2, k), 0.0)
        inv = 1.0 / (1.0 - low - upp - low * ratio)
        ratio = upp * inv
        low_inv = low * inv
        ratio_s[k] = ratio
        low_s[k] = low_inv
        inv_s[k] = inv
        uu, vv = pair(vel, k)
        aa, bb = pair(trc, k)
        wet_inv = jnp.where(wet, inv, 0.0)
        u = (uu + tilt * vv + top_term(k, push_x)) * wet_inv - low_inv * u
        v = (vv - tilt * uu + top_term(k, push_y)) * wet_inv - low_inv * v
        a = (aa + top_term(k, heat)) * wet_inv - low_inv * a
        b = (bb + top_term(k, salt)) * wet_inv - low_inv * b
        val[0, k] = u
        val[1, k] = v
        val[2, k] = a
        val[3, k] = b
        return ratio, u, v, a, b

    sweep(first_forward, (zero, zero, zero, zero, zero), 4)

    def gather_area():
        total = None
        for first, (row_idx, hot) in zip(chunks, cell_maps):
            term = unpack(stage_in(0, first), rows, row_idx, hot)
            total = term if total is None else total + term
        return total

    own_copy.wait()
    receive_copy.wait()
    own_row, own_hot = own_slots()
    cell_maps = [cells(first, chunk) for first in chunks]
    own_vals = pack(payload, 4, own_row, own_hot)
    cell_row, cell_hot = cell_parts(lax.broadcasted_iota(jnp.int32, (1, local), 1))
    own_area = unpack(own_vals, rows, cell_row, cell_hot)
    finish_exchange(0)
    tile = own_area + gather_area()
    sum_tiles = [tile[f * rows : (f + 1) * rows] for f in range(4)]
    start_halo(1, sum_tiles)

    def first_backward(step, carry):
        k = LEV - 1 - step
        u, v, a, b, du, dv = carry
        ratio = ratio_s[k]
        t = at_level(0, k)
        u = val[0, k] - ratio * u
        v = val[1, k] - ratio * v
        a = val[2, k] - ratio * a
        b = val[3, k] - ratio * b
        val[0, k] = u
        val[1, k] = v
        val[2, k] = a
        val[3, k] = b
        return u, v, a, b, du + t * u, dv + t * v

    mixed = sweep(first_backward, (zero,) * 6, 6)
    first_du, first_dv = mixed[4], mixed[5]

    finish_halo(0, state_tiles)
    finish_halo(1, sum_tiles)
    wrows = 5 * rows
    depth_w = win[3]
    rate = transport_rate / LEV
    face_e = jnp.minimum(depth_w, pltpu.roll(depth_w, wrows - 1, 0))
    face_n = jnp.minimum(depth_w, roll_lanes(depth_w, -1))
    filled = depth_w / jnp.maximum(depth_w, depth_floor)
    statics = (rate * face_e, rate * face_n, filled, win[4], win[5], win[6], win[7])
    state = (win[0], roll_lanes(win[0], -1), win[1], win[2])
    shrink = 8
    means = []

    def inner(x):
        return x[shrink : x.shape[0] - shrink]

    for ocean_step in range(STEPS):
        rate_e, rate_n, filled, su, sv, wx, wy = statics
        force_e = coriolis * sv + wx
        force_n = wy - coriolis * su
        push = (rate * force_e, rate * force_n)
        flow_sum = (jnp.zeros_like(force_e), jnp.zeros_like(force_e))
        for part in range(NSUB // shrink):
            rate_e, rate_n = statics[:2]
            push_e, push_n = push
            size = rate_e.shape[0]

            def substep(carry, rate_e=rate_e, rate_n=rate_n, push_e=push_e, push_n=push_n, size=size):
                h, h_next, e, n, te, tn = carry
                e_next = roll_lanes(e, -1)
                h = h - height_rate * (e - pltpu.roll(e, 1, 0) + n - roll_lanes(n, 1))
                h_next = h_next - height_rate * (
                    e_next - pltpu.roll(e_next, 1, 0) + roll_lanes(n, -1) - n
                )
                slope_e = pltpu.roll(h, size - 1, 0) - h
                slope_n = h_next - h
                e = jnp.where(rate_e > 0, e + (push_e - rate_e * slope_e), 0.0)
                n = jnp.where(rate_n > 0, n + (push_n - rate_n * slope_n), 0.0)
                return h, h_next, e, n, te + e, tn + n

            def two(counter, carry, substep=substep):
                return substep(substep(carry))

            carry = lax.fori_loop(0, shrink // 2, two, state + flow_sum)
            carry = tuple(inner(x) for x in carry)
            statics = tuple(inner(x) for x in statics)
            push = tuple(inner(x) for x in push)
            state, flow_sum = carry[:4], carry[4:]
        mean_e = flow_sum[0] / NSUB
        mean_n = flow_sum[1] / NSUB
        means += [mean_e, mean_n]
        if ocean_step + 1 < STEPS:
            rate_e, rate_n, filled, su, sv, wx, wy = statics
            du = su + time_step * (coriolis * sv + wx)
            dv = sv + time_step * (wy - coriolis * su)
            su = du + (mean_e - du) * filled
            sv = dv + (mean_n - dv) * filled
            statics = (rate_e, rate_n, filled, su, sv, wx, wy)

    def centre(x):
        first = (x.shape[0] - rows) // 2
        return roll_lanes(x[first : first + rows], -HALO)

    flow = jnp.concatenate([centre(x) for x in means], axis=0)
    for first, (row_idx, hot) in zip(chunks, cell_maps):
        stage_out(1, first, pack(flow, 4, row_idx, hot))
    start_exchange(1)
    def second_forward(k, carry):
        u, v, a, b = carry
        low_inv = low_s[k]
        wet_inv = jnp.where(lev > k, inv_s[k], 0.0)
        uu = val[0, k]
        vv = val[1, k]
        u = (uu + tilt * vv + top_term(k, push_x)) * wet_inv - low_inv * u
        v = (vv - tilt * uu + top_term(k, push_y)) * wet_inv - low_inv * v
        a = (val[2, k] + top_term(k, heat)) * wet_inv - low_inv * a
        b = (val[3, k] + top_term(k, salt)) * wet_inv - low_inv * b
        val[0, k] = u
        val[1, k] = v
        val[2, k] = a
        val[3, k] = b
        return u, v, a, b

    sweep(second_forward, (zero,) * 4, 6)

    def second_backward(step, carry):
        k = LEV - 1 - step
        u, v, a, b, du, dv = carry
        ratio = ratio_s[k]
        t = at_level(0, k)
        u = val[0, k] - ratio * u
        v = val[1, k] - ratio * v
        a = val[2, k] - ratio * a
        b = val[3, k] - ratio * b
        val[0, k] = u
        val[1, k] = v
        put_pair(trc, k, a, b)
        return u, v, a, b, du + t * u, dv + t * v

    mixed = sweep(second_backward, (zero,) * 6, 6)
    second_du, second_dv = mixed[4], mixed[5]

    out_trc[...] = trc[...].astype(jnp.bfloat16)
    out_height[...] = centre(state[0])[:, :cols]
    out_transport[0] = centre(state[2])[:, :cols]
    out_transport[1] = centre(state[3])[:, :cols]
    slot_flow = unpack(pack(flow, 4, cell_row, cell_hot), brows, own_row, own_hot)
    finish_exchange(1)
    for first, (row_idx, hot) in zip(chunks, slot_maps):
        slot_flow = slot_flow + unpack(stage_in(1, first), brows, row_idx, hot)

    floor = jnp.maximum(depth, depth_floor)
    shift_u = (slot_flow[0:brows] - first_du) / floor
    shift_v = (slot_flow[brows : 2 * brows] - first_dv) / floor
    carry_u = shift_u + tilt * shift_v
    carry_v = shift_v - tilt * shift_u
    last_u = carry_u + (slot_flow[2 * brows : 3 * brows] - second_du - depth * carry_u) / floor
    last_v = carry_v + (slot_flow[3 * brows :] - second_dv - depth * carry_v) / floor

    def finish(k, carry):
        wet = lev > k
        put_pair(
            vel,
            k,
            val[0, k] + jnp.where(wet, last_u, 0.0),
            val[1, k] + jnp.where(wet, last_v, 0.0),
        )
        return carry

    sweep(finish, 0, 6)
    out_vel[...] = vel[...].astype(jnp.bfloat16)


def deliver(*refs):
    count = (len(refs) - 1) // 2
    sems = refs[-1]
    copies = [
        pltpu.make_async_copy(refs[i], refs[count + i], sems.at[i]) for i in range(count)
    ]
    for copy in copies:
        copy.start()
    for copy in copies:
        copy.wait()


def flat(x, brows):
    x = x.reshape(2, LEV, brows, LANES)
    return jnp.transpose(x, (1, 2, 0, 3)).reshape(LEV * brows * 2, LANES)


def unflat(x, brows):
    x = x.reshape(LEV, brows, 2, LANES)
    return jnp.transpose(x, (2, 0, 1, 3)).reshape(2, LEV, 1, brows * LANES)


def body(
    n_tx,
    n_ty,
    velocity,
    tracers,
    surface_forcing,
    thickness,
    levels,
    surface_levels,
    height,
    transport,
    send_list,
    receive_cell,
    own_slot,
):
    rows, cols = height.shape
    slots = levels.shape[1]
    brows = slots // LANES
    cap = send_list.shape[3]
    forcing = surface_forcing.reshape(4, brows, LANES)
    pad = ((0, 0), (0, 0), (0, LANES - cap))
    sends, receives = send_list[0], receive_cell[0]
    if cap < LANES:
        sends = jnp.pad(sends, pad, constant_values=-1)
        receives = jnp.pad(receives, pad, constant_values=-1)
    operands = (
        thickness.reshape(1, LEV),
        flat(velocity, brows),
        flat(tracers, brows),
        forcing,
        levels.reshape(brows, LANES),
        surface_levels,
        height,
        transport,
        sends[0],
        receives[0],
        own_slot,
    )
    vmem = pl.BlockSpec(memory_space=pltpu.VMEM)
    hbm = pl.BlockSpec(memory_space=pltpu.HBM)
    f32 = jnp.float32
    column = pltpu.VMEM((LEV, brows, LANES), f32)
    whole = (LEV * brows * 2, LANES)
    results = (
        jax.ShapeDtypeStruct(whole, jnp.bfloat16),
        jax.ShapeDtypeStruct(whole, jnp.bfloat16),
        jax.ShapeDtypeStruct((rows, cols), f32),
        jax.ShapeDtypeStruct((2, rows, cols), f32),
    )
    got = pl.pallas_call(
        functools.partial(kernel, n_tx, n_ty),
        out_shape=results,
        in_specs=[hbm] * len(operands),
        out_specs=(vmem,) * 4,
        scratch_shapes=[pltpu.VMEM(x.shape, x.dtype) for x in operands]
        + [
            pltpu.SemaphoreType.DMA((len(operands),)),
            pltpu.VMEM((3, 64, LANES), f32),
            pltpu.VMEM(whole, f32),
            pltpu.VMEM(whole, f32),
            column,
            column,
            column,
            pltpu.VMEM((4, LEV, brows, LANES), f32),
            pltpu.VMEM((2, n_tx, 4, LANES), f32),
            pltpu.VMEM((2, n_tx, 4, LANES), f32),
            pltpu.VMEM((2, 2, rows, LANES), f32),
            pltpu.VMEM((2, rows, LANES), f32),
            pltpu.VMEM((2, rows, LANES), f32),
            pltpu.VMEM((2, 5, 2, rows, LANES), f32),
            pltpu.VMEM((2, 5, 2, rows, LANES), f32),
            pltpu.VMEM((8, 5 * rows, LANES), f32),
            pltpu.SemaphoreType.DMA((2, n_tx)),
            pltpu.SemaphoreType.DMA((2, n_tx)),
            pltpu.SemaphoreType.DMA((2, 15)),
            pltpu.SemaphoreType.DMA((2, 15)),
        ],
        compiler_params=pltpu.CompilerParams(
            collective_id=0, has_side_effects=True, vmem_limit_bytes=48 * 1024 * 1024
        ),
        name="ocean",
    )(*[pltpu.with_memory_space_constraint(x, pltpu.HBM) for x in operands])
    new_vel, new_trc, new_height, new_transport = pl.pallas_call(
        deliver,
        out_shape=results,
        in_specs=[vmem] * 4,
        out_specs=(hbm,) * 4,
        scratch_shapes=[pltpu.SemaphoreType.DMA((4,))],
        name="deliver",
    )(*[pltpu.with_memory_space_constraint(x, pltpu.VMEM) for x in got])
    return (unflat(new_vel, brows), unflat(new_trc, brows), new_height, new_transport)


def solution(mesh):
    in_specs = (
        P(None, None, "ty", "tx"),
        P(None, None, "ty", "tx"),
        P(None, "ty", "tx"),
        P(),
        P("ty", "tx"),
        P("tx", "ty"),
        P("tx", "ty"),
        P(None, "tx", "ty"),
        P("ty", "tx", None, None),
        P("ty", "tx", None, None),
        P("tx", "ty"),
    )
    out_specs = (
        P(None, None, "ty", "tx"),
        P(None, None, "ty", "tx"),
        P("tx", "ty"),
        P(None, "tx", "ty"),
    )
    return jax.shard_map(
        functools.partial(body, mesh.shape["tx"], mesh.shape["ty"]),
        mesh=mesh,
        in_specs=in_specs,
        out_specs=out_specs,
        check_vma=False,
    )
```

```python
import functools

import jax
import jax.numpy as jnp
from jax import lax
from jax.experimental import pallas as pl
from jax.experimental.pallas import tpu as pltpu
from jax.sharding import PartitionSpec as P

LEV = 60
NSUB = 16
STEPS = 2

time_step = 0.5
coriolis = 0.3
mixing = 200.0
height_rate = 0.25
transport_rate = 0.9
depth_floor = 1.0

LANES = 128
HALO = NSUB * STEPS
OFFSETS = [(dx, dy) for dx in (-2, -1, 0, 1, 2) for dy in (-1, 0, 1) if (dx, dy) != (0, 0)]


def slot_of(dx, dy):
    return (dx + 2) * 3 + dy + 1


def split3(x):
    high = x.astype(jnp.bfloat16)
    rest = x - high.astype(jnp.float32)
    mid = rest.astype(jnp.bfloat16)
    low = (rest - mid.astype(jnp.float32)).astype(jnp.bfloat16)
    return high, mid, low


def one_hot(lane_idx):
    shape = (LANES, lane_idx.shape[1])
    hit = lax.broadcasted_iota(jnp.int32, shape, 0) == lane_idx
    return jnp.where(hit, 1.0, 0.0).astype(jnp.bfloat16)


def pack(values, count, row_idx, hot):
    rows = values.shape[0] // count
    entries = hot.shape[1]
    got = None
    for part in split3(values):
        term = jnp.dot(part, hot, preferred_element_type=jnp.float32)
        got = term if got is None else got + term
    got = got.reshape(count, rows, entries)
    hit = lax.broadcasted_iota(jnp.int32, (1, rows, entries), 1) == row_idx[None]
    return jnp.sum(jnp.where(hit, got, 0.0), axis=1)


def unpack(entries, rows, row_idx, hot):
    count, size = entries.shape
    hit = lax.broadcasted_iota(jnp.int32, (1, rows, size), 1) == row_idx[None]
    total = None
    for part in split3(entries):
        spread = jnp.where(hit, part.astype(jnp.float32)[:, None, :], 0.0)
        spread = spread.reshape(count * rows, size).astype(jnp.bfloat16)
        term = lax.dot_general(
            spread, hot, (((1,), (1,)), ((), ())), preferred_element_type=jnp.float32
        )
        total = term if total is None else total + term
    return total


def kernel(
    n_tx,
    n_ty,
    thick_hbm,
    vel_hbm,
    trc_hbm,
    forcing_hbm,
    levels_hbm,
    area_levels_hbm,
    height_hbm,
    transport_hbm,
    send_hbm,
    receive_hbm,
    own_hbm,
    out_vel,
    out_trc,
    out_height,
    out_transport,
    thick_in,
    vel_in,
    trc_in,
    forcing,
    levels,
    area_levels_in,
    height_in,
    transport_in,
    send_in,
    receive_in,
    own_in,
    in_sem,
    coef,
    vel,
    trc,
    low_s,
    inv_s,
    ratio_s,
    val,
    a2a_out,
    a2a_in,
    pair_out,
    right_out,
    left_out,
    pair_in,
    side_in,
    win,
    a2a_send,
    a2a_recv,
    halo_send,
    halo_recv,
):
    tx = lax.axis_index("tx")
    ty = lax.axis_index("ty")
    rows = height_in.shape[0]
    cols = LANES - 2 * HALO
    brows = forcing.shape[1]
    remote = n_tx * LANES
    local = rows * cols

    def present(dx, dy):
        return (tx + dx >= 0) & (tx + dx < n_tx) & (ty + dy >= 0) & (ty + dy < n_ty)

    def fetch(number, src, dst):
        copy = pltpu.make_async_copy(src, dst, in_sem.at[number])
        copy.start()
        return copy

    vel_copy = fetch(0, vel_hbm, vel_in)
    thick_copy = fetch(1, thick_hbm, thick_in)
    level_copy = fetch(2, levels_hbm, levels)
    area_level_copy = fetch(3, area_levels_hbm, area_levels_in)
    forcing_copy = fetch(4, forcing_hbm, forcing)
    send_copy = fetch(5, send_hbm, send_in)
    height_copy = fetch(6, height_hbm, height_in)
    transport_copy = fetch(7, transport_hbm, transport_in)
    trc_copy = fetch(8, trc_hbm, trc_in)
    receive_copy = fetch(9, receive_hbm, receive_in)
    own_copy = fetch(10, own_hbm, own_in)

    barrier = pltpu.get_barrier_semaphore()

    def greet(step, carry):
        pl.semaphore_signal(
            barrier,
            inc=1,
            device_id={"tx": lax.rem(tx + step, n_tx), "ty": ty},
            device_id_type=pl.DeviceIdType.MESH,
        )
        return carry

    a2a_in[...] = jnp.zeros_like(a2a_in)
    pair_in[...] = jnp.zeros_like(pair_in)
    side_in[...] = jnp.zeros_like(side_in)

    lax.fori_loop(1, n_tx, greet, 0)
    for dx, dy in OFFSETS:
        if dy != 0:

            @pl.when(present(dx, dy))
            def _():
                pl.semaphore_signal(
                    barrier,
                    inc=1,
                    device_id={"tx": tx + dx, "ty": ty + dy},
                    device_id_type=pl.DeviceIdType.MESH,
                )

    thick_copy.wait()
    size = coef.shape[1]
    row_at = lax.broadcasted_iota(jnp.int32, (size, LANES), 0)
    lane_at = lax.broadcasted_iota(jnp.int32, (size, LANES), 1)
    row = thick_in[...]
    row = jnp.concatenate([row, jnp.ones((1, LANES - LEV), jnp.float32)], axis=1)

    def along_rows(x):
        column = jnp.sum(jnp.where(row_at == lane_at, x, 0.0), axis=1, keepdims=True)
        return jnp.broadcast_to(column, (size, LANES))

    thick = along_rows(row)
    gap = jnp.where(
        lane_at[:1] < LEV - 1, mixing / (row + pltpu.roll(row, LANES - 1, 1)), 0.0
    )
    coef[0] = thick
    coef[1] = along_rows(pltpu.roll(gap, 1, 1)) / thick
    coef[2] = along_rows(gap) / thick

    def at_level(which, k):
        return jnp.broadcast_to(coef[which, pl.ds(k, 1), :], (brows, LANES))

    def pair(ref, k):
        first = pl.multiple_of(k * 2 * brows, 2 * brows)
        return (
            ref[pl.ds(first, brows, stride=2), :],
            ref[pl.ds(first + 1, brows, stride=2), :],
        )

    def put_pair(ref, k, one, two):
        first = pl.multiple_of(k * 2 * brows, 2 * brows)
        ref[pl.ds(first, brows, stride=2), :] = one
        ref[pl.ds(first + 1, brows, stride=2), :] = two

    def sweep(step, carry, unroll):
        def several(block, inner):
            for sub in range(unroll):
                inner = step(block * unroll + sub, inner)
            return inner

        return lax.fori_loop(0, LEV // unroll, several, carry)

    level_copy.wait()
    area_level_copy.wait()
    lev = levels[...]
    wet0 = lev > 0

    def widen(x):
        return jnp.concatenate([x, jnp.zeros((rows, LANES - cols), x.dtype)], axis=1)

    area_lev = widen(area_levels_in[...])
    vel_copy.wait()
    vel[...] = vel_in[...].astype(jnp.float32)

    def add_level(k, carry):
        su, sv, depth, area_depth = carry
        t = at_level(0, k)
        wet = jnp.where(lev > k, t, 0.0)
        uu, vv = pair(vel, k)
        su = su + wet * uu
        sv = sv + wet * vv
        t = jnp.broadcast_to(coef[0, pl.ds(k, 1), :], (rows, LANES))
        area_depth = area_depth + jnp.where(area_lev > k, t, 0.0)
        return su, sv, depth + wet, area_depth

    zero = jnp.zeros((brows, LANES), jnp.float32)
    sum_u, sum_v, depth, area_depth = sweep(
        add_level, (zero, zero, zero, jnp.zeros((rows, LANES), jnp.float32)), 6
    )
    forcing_copy.wait()
    wind_x = jnp.where(wet0, forcing[0], 0.0)
    wind_y = jnp.where(wet0, forcing[1], 0.0)
    payload = jnp.concatenate([sum_u, sum_v, wind_x, wind_y], axis=0)

    def by_lanes(x):
        return jnp.concatenate([x[r : r + 1] for r in range(x.shape[0])], axis=1)

    def slots(start, size):
        idx = by_lanes(send_in[start // LANES : (start + size) // LANES, :])
        return idx >> 7, one_hot(idx & (LANES - 1))

    def own_slots():
        halves = LANES // cols
        got = [own_in[pl.ds(h, rows // halves, stride=halves), :] for h in range(halves)]
        idx = by_lanes(jnp.concatenate(got, axis=1))
        return idx >> 7, one_hot(idx & (LANES - 1))

    def cell_parts(idx):
        return lax.div(idx + cols, cols) - 1, one_hot(lax.rem(idx + cols, cols))

    def cells(start, size):
        return cell_parts(by_lanes(receive_in[start // LANES : (start + size) // LANES, :]))

    chunk = min(1024, remote)
    per_chunk = chunk // LANES
    chunks = range(0, remote, chunk)

    def exchange_copy(stage, peer, mine):
        return pltpu.make_async_remote_copy(
            src_ref=a2a_out.at[stage, peer],
            dst_ref=a2a_in.at[stage, mine],
            send_sem=a2a_send.at[stage, peer],
            recv_sem=a2a_recv.at[stage, mine],
            device_id={"tx": peer, "ty": ty},
            device_id_type=pl.DeviceIdType.MESH,
        )

    def start_exchange(stage):
        def go(step, carry):
            exchange_copy(stage, lax.rem(tx + step, n_tx), tx).start()
            return carry

        lax.fori_loop(1, n_tx, go, 0)

    def finish_exchange(stage):
        def go(step, carry):
            exchange_copy(stage, lax.rem(tx + step, n_tx), tx).wait_send()
            source = lax.rem(tx + step, n_tx)
            exchange_copy(stage, source, source).wait_recv()
            return carry

        lax.fori_loop(1, n_tx, go, 0)

    def stage_out(stage, first, packed):
        for block in range(per_chunk):
            a2a_out[stage, first // LANES + block] = packed[:, block * LANES : (block + 1) * LANES]

    def stage_in(stage, first):
        return jnp.concatenate(
            [a2a_in[stage, first // LANES + block] for block in range(per_chunk)], axis=1
        )

    send_copy.wait()
    slot_maps = [slots(first, chunk) for first in chunks]
    for first, (row_idx, hot) in zip(chunks, slot_maps):
        stage_out(0, first, pack(payload, 4, row_idx, hot))

    greeted = jnp.int32(n_tx - 1)
    for dx, dy in OFFSETS:
        if dy != 0:
            greeted = greeted + jnp.where(present(dx, dy), 1, 0)
    pl.semaphore_wait(barrier, greeted)
    start_exchange(0)

    lane = lax.broadcasted_iota(jnp.int32, (rows, LANES), 1)

    def halo_copy(stage, dx, dy):
        there = slot_of(-dx, -dy)
        if dy == 0:
            src, dst = pair_out.at[stage], pair_in.at[stage, 2 - dx]
        else:
            src = (right_out if dy > 0 else left_out).at[stage]
            dst = side_in.at[stage, 2 - dx, 0 if dy > 0 else 1]
        return pltpu.make_async_remote_copy(
            src_ref=src,
            dst_ref=dst,
            send_sem=halo_send.at[stage, slot_of(dx, dy)],
            recv_sem=halo_recv.at[stage, there],
            device_id={"tx": tx + dx, "ty": ty + dy},
            device_id_type=pl.DeviceIdType.MESH,
        )

    def start_halo(stage, tiles):
        for half in range(2):
            pair_out[stage, half] = jnp.where(
                lane < cols, tiles[2 * half], pltpu.roll(tiles[2 * half + 1], cols, 1)
            )
        right = jnp.zeros((rows, LANES), jnp.float32)
        left = jnp.zeros((rows, LANES), jnp.float32)
        for f in range(4):
            here = (lane >= HALO * f) & (lane < HALO * (f + 1))
            shift = (HALO * f - (cols - HALO)) % LANES
            right = jnp.where(here, pltpu.roll(tiles[f], shift, 1) if shift else tiles[f], right)
            shift = HALO * f
            left = jnp.where(here, pltpu.roll(tiles[f], shift, 1) if shift else tiles[f], left)
        right_out[stage] = right
        left_out[stage] = left
        for dx, dy in OFFSETS:

            @pl.when(present(dx, dy))
            def _():
                halo_copy(stage, dx, dy).start()

    def roll_lanes(x, shift):
        shift = shift % LANES
        return pltpu.roll(x, shift, 1) if shift else x

    def finish_halo(stage, tiles):
        for dx, dy in OFFSETS:

            @pl.when(present(dx, dy))
            def _():
                halo_copy(stage, dx, dy).wait_send()
                halo_copy(stage, -dx, -dy).wait_recv()

        for dx in (-2, -1, 0, 1, 2):
            from_left = side_in[stage, dx + 2, 0]
            from_right = side_in[stage, dx + 2, 1]
            for f in range(4):
                if dx == 0:
                    middle = roll_lanes(tiles[f], HALO)
                else:
                    pair = pair_in[stage, dx + 2, f // 2]
                    middle = roll_lanes(pair, HALO if f % 2 == 0 else HALO - cols)
                block = jnp.where(
                    lane < HALO,
                    roll_lanes(from_left, -HALO * f),
                    jnp.where(
                        lane >= HALO + cols,
                        roll_lanes(from_right, HALO + cols - HALO * f),
                        middle,
                    ),
                )
                win[stage * 4 + f, (dx + 2) * rows : (dx + 3) * rows, :] = block

    height_copy.wait()
    transport_copy.wait()
    state_tiles = [
        widen(height_in[...]),
        widen(transport_in[0]),
        widen(transport_in[1]),
        area_depth,
    ]
    start_halo(0, state_tiles)

    trc_copy.wait()
    trc[...] = trc_in[...].astype(jnp.float32)
    inv_top = 1.0 / at_level(0, 0)
    heat = jnp.where(wet0, time_step * inv_top * forcing[2], 0.0)
    salt = jnp.where(wet0, time_step * inv_top * forcing[3], 0.0)
    push_x = time_step * inv_top * wind_x
    push_y = time_step * inv_top * wind_y
    tilt = time_step * coriolis

    def top_term(k, x):
        return jnp.where(k == 0, x, 0.0)

    def coefficients(k, ratio):
        low = jnp.where(lev > k, -at_level(1, k), 0.0)
        upp = jnp.where(lev > k + 1, -at_level(2, k), 0.0)
        inv = 1.0 / (1.0 - low - upp - low * ratio)
        ratio = upp * inv
        ratio_s[k] = ratio
        low_s[k] = low * inv
        inv_s[k] = inv
        return ratio

    sweep(coefficients, zero, 6)

    def gather_area():
        total = None
        for first, (row_idx, hot) in zip(chunks, cell_maps):
            term = unpack(stage_in(0, first), rows, row_idx, hot)
            total = term if total is None else total + term
        return total

    own_copy.wait()
    receive_copy.wait()
    own_row, own_hot = own_slots()
    cell_maps = [cells(first, chunk) for first in chunks]
    own_vals = pack(payload, 4, own_row, own_hot)
    cell_row, cell_hot = cell_parts(lax.broadcasted_iota(jnp.int32, (1, local), 1))
    own_area = unpack(own_vals, rows, cell_row, cell_hot)
    finish_exchange(0)
    tile = own_area + gather_area()
    sum_tiles = [tile[f * rows : (f + 1) * rows] for f in range(4)]
    start_halo(1, sum_tiles)

    finish_halo(0, state_tiles)

    def first_forward(k, carry):
        u, v, a, b = carry
        low_inv = low_s[k]
        wet_inv = jnp.where(lev > k, inv_s[k], 0.0)
        uu, vv = pair(vel, k)
        aa, bb = pair(trc, k)
        u = (uu + tilt * vv + top_term(k, push_x)) * wet_inv - low_inv * u
        v = (vv - tilt * uu + top_term(k, push_y)) * wet_inv - low_inv * v
        a = (aa + top_term(k, heat)) * wet_inv - low_inv * a
        b = (bb + top_term(k, salt)) * wet_inv - low_inv * b
        val[0, k] = u
        val[1, k] = v
        val[2, k] = a
        val[3, k] = b
        return u, v, a, b

    sweep(first_forward, (zero,) * 4, 6)

    def first_backward(step, carry):
        k = LEV - 1 - step
        u, v, a, b, du, dv = carry
        ratio = ratio_s[k]
        t = at_level(0, k)
        u = val[0, k] - ratio * u
        v = val[1, k] - ratio * v
        a = val[2, k] - ratio * a
        b = val[3, k] - ratio * b
        val[0, k] = u
        val[1, k] = v
        val[2, k] = a
        val[3, k] = b
        return u, v, a, b, du + t * u, dv + t * v

    mixed = sweep(first_backward, (zero,) * 6, 6)
    first_du, first_dv = mixed[4], mixed[5]

    finish_halo(1, sum_tiles)
    wrows = 5 * rows
    depth_w = win[3]
    rate = transport_rate / LEV
    face_e = jnp.minimum(depth_w, pltpu.roll(depth_w, wrows - 1, 0))
    face_n = jnp.minimum(depth_w, roll_lanes(depth_w, -1))
    filled = depth_w / jnp.maximum(depth_w, depth_floor)
    statics = (rate * face_e, rate * face_n, filled, win[4], win[5], win[6], win[7])
    state = (win[0], roll_lanes(win[0], -1), win[1], win[2])
    shrink = 8
    means = []

    def inner(x):
        return x[shrink : x.shape[0] - shrink]

    for ocean_step in range(STEPS):
        rate_e, rate_n, filled, su, sv, wx, wy = statics
        force_e = coriolis * sv + wx
        force_n = wy - coriolis * su
        push = (rate * force_e, rate * force_n)
        flow_sum = (jnp.zeros_like(force_e), jnp.zeros_like(force_e))
        for part in range(NSUB // shrink):
            rate_e, rate_n = statics[:2]
            push_e, push_n = push
            size = rate_e.shape[0]

            def substep(carry, rate_e=rate_e, rate_n=rate_n, push_e=push_e, push_n=push_n, size=size):
                h, h_next, e, n, te, tn = carry
                e_next = roll_lanes(e, -1)
                h = h - height_rate * (e - pltpu.roll(e, 1, 0) + n - roll_lanes(n, 1))
                h_next = h_next - height_rate * (
                    e_next - pltpu.roll(e_next, 1, 0) + roll_lanes(n, -1) - n
                )
                slope_e = pltpu.roll(h, size - 1, 0) - h
                slope_n = h_next - h
                e = jnp.where(rate_e > 0, e + (push_e - rate_e * slope_e), 0.0)
                n = jnp.where(rate_n > 0, n + (push_n - rate_n * slope_n), 0.0)
                return h, h_next, e, n, te + e, tn + n

            def four(counter, carry, substep=substep):
                return substep(substep(substep(substep(carry))))

            carry = lax.fori_loop(0, shrink // 4, four, state + flow_sum)
            carry = tuple(inner(x) for x in carry)
            statics = tuple(inner(x) for x in statics)
            push = tuple(inner(x) for x in push)
            state, flow_sum = carry[:4], carry[4:]
        mean_e = flow_sum[0] / NSUB
        mean_n = flow_sum[1] / NSUB
        means += [mean_e, mean_n]
        if ocean_step + 1 < STEPS:
            rate_e, rate_n, filled, su, sv, wx, wy = statics
            du = su + time_step * (coriolis * sv + wx)
            dv = sv + time_step * (wy - coriolis * su)
            su = du + (mean_e - du) * filled
            sv = dv + (mean_n - dv) * filled
            statics = (rate_e, rate_n, filled, su, sv, wx, wy)

    def centre(x):
        first = (x.shape[0] - rows) // 2
        return roll_lanes(x[first : first + rows], -HALO)

    flow = jnp.concatenate([centre(x) for x in means], axis=0)
    for first, (row_idx, hot) in zip(chunks, cell_maps):
        stage_out(1, first, pack(flow, 4, row_idx, hot))
    start_exchange(1)
    def second_forward(k, carry):
        u, v, a, b = carry
        low_inv = low_s[k]
        wet_inv = jnp.where(lev > k, inv_s[k], 0.0)
        uu = val[0, k]
        vv = val[1, k]
        u = (uu + tilt * vv + top_term(k, push_x)) * wet_inv - low_inv * u
        v = (vv - tilt * uu + top_term(k, push_y)) * wet_inv - low_inv * v
        a = (val[2, k] + top_term(k, heat)) * wet_inv - low_inv * a
        b = (val[3, k] + top_term(k, salt)) * wet_inv - low_inv * b
        val[0, k] = u
        val[1, k] = v
        val[2, k] = a
        val[3, k] = b
        return u, v, a, b

    sweep(second_forward, (zero,) * 4, 6)

    def second_backward(step, carry):
        k = LEV - 1 - step
        u, v, a, b, du, dv = carry
        ratio = ratio_s[k]
        t = at_level(0, k)
        u = val[0, k] - ratio * u
        v = val[1, k] - ratio * v
        a = val[2, k] - ratio * a
        b = val[3, k] - ratio * b
        val[0, k] = u
        val[1, k] = v
        put_pair(trc, k, a, b)
        return u, v, a, b, du + t * u, dv + t * v

    mixed = sweep(second_backward, (zero,) * 6, 6)
    second_du, second_dv = mixed[4], mixed[5]

    out_trc[...] = trc[...].astype(jnp.bfloat16)
    out_height[...] = centre(state[0])[:, :cols]
    out_transport[0] = centre(state[2])[:, :cols]
    out_transport[1] = centre(state[3])[:, :cols]
    slot_flow = unpack(pack(flow, 4, cell_row, cell_hot), brows, own_row, own_hot)
    finish_exchange(1)
    for first, (row_idx, hot) in zip(chunks, slot_maps):
        slot_flow = slot_flow + unpack(stage_in(1, first), brows, row_idx, hot)

    floor = jnp.maximum(depth, depth_floor)
    shift_u = (slot_flow[0:brows] - first_du) / floor
    shift_v = (slot_flow[brows : 2 * brows] - first_dv) / floor
    carry_u = shift_u + tilt * shift_v
    carry_v = shift_v - tilt * shift_u
    last_u = carry_u + (slot_flow[2 * brows : 3 * brows] - second_du - depth * carry_u) / floor
    last_v = carry_v + (slot_flow[3 * brows :] - second_dv - depth * carry_v) / floor

    def finish(k, carry):
        wet = lev > k
        put_pair(
            vel,
            k,
            val[0, k] + jnp.where(wet, last_u, 0.0),
            val[1, k] + jnp.where(wet, last_v, 0.0),
        )
        return carry

    sweep(finish, 0, 6)
    out_vel[...] = vel[...].astype(jnp.bfloat16)


def deliver(*refs):
    count = (len(refs) - 1) // 2
    sems = refs[-1]
    copies = [
        pltpu.make_async_copy(refs[i], refs[count + i], sems.at[i]) for i in range(count)
    ]
    for copy in copies:
        copy.start()
    for copy in copies:
        copy.wait()


def flat(x, brows):
    x = x.reshape(2, LEV, brows, LANES)
    return jnp.transpose(x, (1, 2, 0, 3)).reshape(LEV * brows * 2, LANES)


def unflat(x, brows):
    x = x.reshape(LEV, brows, 2, LANES)
    return jnp.transpose(x, (2, 0, 1, 3)).reshape(2, LEV, 1, brows * LANES)


def body(
    n_tx,
    n_ty,
    velocity,
    tracers,
    surface_forcing,
    thickness,
    levels,
    surface_levels,
    height,
    transport,
    send_list,
    receive_cell,
    own_slot,
):
    rows, cols = height.shape
    slots = levels.shape[1]
    brows = slots // LANES
    cap = send_list.shape[3]
    forcing = surface_forcing.reshape(4, brows, LANES)
    pad = ((0, 0), (0, 0), (0, LANES - cap))
    sends, receives = send_list[0], receive_cell[0]
    if cap < LANES:
        sends = jnp.pad(sends, pad, constant_values=-1)
        receives = jnp.pad(receives, pad, constant_values=-1)
    operands = (
        thickness.reshape(1, LEV),
        flat(velocity, brows),
        flat(tracers, brows),
        forcing,
        levels.reshape(brows, LANES),
        surface_levels,
        height,
        transport,
        sends[0],
        receives[0],
        own_slot,
    )
    vmem = pl.BlockSpec(memory_space=pltpu.VMEM)
    hbm = pl.BlockSpec(memory_space=pltpu.HBM)
    f32 = jnp.float32
    column = pltpu.VMEM((LEV, brows, LANES), f32)
    whole = (LEV * brows * 2, LANES)
    results = (
        jax.ShapeDtypeStruct(whole, jnp.bfloat16),
        jax.ShapeDtypeStruct(whole, jnp.bfloat16),
        jax.ShapeDtypeStruct((rows, cols), f32),
        jax.ShapeDtypeStruct((2, rows, cols), f32),
    )
    got = pl.pallas_call(
        functools.partial(kernel, n_tx, n_ty),
        out_shape=results,
        in_specs=[hbm] * len(operands),
        out_specs=(vmem,) * 4,
        scratch_shapes=[pltpu.VMEM(x.shape, x.dtype) for x in operands]
        + [
            pltpu.SemaphoreType.DMA((len(operands),)),
            pltpu.VMEM((3, 64, LANES), f32),
            pltpu.VMEM(whole, f32),
            pltpu.VMEM(whole, f32),
            column,
            column,
            column,
            pltpu.VMEM((4, LEV, brows, LANES), f32),
            pltpu.VMEM((2, n_tx, 4, LANES), f32),
            pltpu.VMEM((2, n_tx, 4, LANES), f32),
            pltpu.VMEM((2, 2, rows, LANES), f32),
            pltpu.VMEM((2, rows, LANES), f32),
            pltpu.VMEM((2, rows, LANES), f32),
            pltpu.VMEM((2, 5, 2, rows, LANES), f32),
            pltpu.VMEM((2, 5, 2, rows, LANES), f32),
            pltpu.VMEM((8, 5 * rows, LANES), f32),
            pltpu.SemaphoreType.DMA((2, n_tx)),
            pltpu.SemaphoreType.DMA((2, n_tx)),
            pltpu.SemaphoreType.DMA((2, 15)),
            pltpu.SemaphoreType.DMA((2, 15)),
        ],
        compiler_params=pltpu.CompilerParams(
            collective_id=0, has_side_effects=True, vmem_limit_bytes=48 * 1024 * 1024
        ),
        name="ocean",
    )(*[pltpu.with_memory_space_constraint(x, pltpu.HBM) for x in operands])
    new_vel, new_trc, new_height, new_transport = pl.pallas_call(
        deliver,
        out_shape=results,
        in_specs=[vmem] * 4,
        out_specs=(hbm,) * 4,
        scratch_shapes=[pltpu.SemaphoreType.DMA((4,))],
        name="deliver",
    )(*[pltpu.with_memory_space_constraint(x, pltpu.VMEM) for x in got])
    return (unflat(new_vel, brows), unflat(new_trc, brows), new_height, new_transport)


def solution(mesh):
    in_specs = (
        P(None, None, "ty", "tx"),
        P(None, None, "ty", "tx"),
        P(None, "ty", "tx"),
        P(),
        P("ty", "tx"),
        P("tx", "ty"),
        P("tx", "ty"),
        P(None, "tx", "ty"),
        P("ty", "tx", None, None),
        P("ty", "tx", None, None),
        P("tx", "ty"),
    )
    out_specs = (
        P(None, None, "ty", "tx"),
        P(None, None, "ty", "tx"),
        P("tx", "ty"),
        P(None, "tx", "ty"),
    )
    return jax.shard_map(
        functools.partial(body, mesh.shape["tx"], mesh.shape["ty"]),
        mesh=mesh,
        in_specs=in_specs,
        out_specs=out_specs,
        check_vma=False,
    )
```

```python
import functools

import jax
import jax.numpy as jnp
from jax import lax
from jax.experimental import pallas as pl
from jax.experimental.pallas import tpu as pltpu
from jax.sharding import PartitionSpec as P

LEV = 60
NSUB = 16
STEPS = 2

time_step = 0.5
coriolis = 0.3
mixing = 200.0
height_rate = 0.25
transport_rate = 0.9
depth_floor = 1.0

LANES = 128
HALO = NSUB * STEPS
OFFSETS = [(dx, dy) for dx in (-2, -1, 0, 1, 2) for dy in (-1, 0, 1) if (dx, dy) != (0, 0)]


def slot_of(dx, dy):
    return (dx + 2) * 3 + dy + 1


def split3(x):
    high = x.astype(jnp.bfloat16)
    rest = x - high.astype(jnp.float32)
    mid = rest.astype(jnp.bfloat16)
    low = (rest - mid.astype(jnp.float32)).astype(jnp.bfloat16)
    return high, mid, low


def one_hot(lane_idx):
    shape = (LANES, lane_idx.shape[1])
    hit = lax.broadcasted_iota(jnp.int32, shape, 0) == lane_idx
    return jnp.where(hit, 1.0, 0.0).astype(jnp.bfloat16)


def pack(values, count, row_idx, hot):
    rows = values.shape[0] // count
    entries = hot.shape[1]
    got = None
    for part in split3(values):
        term = jnp.dot(part, hot, preferred_element_type=jnp.float32)
        got = term if got is None else got + term
    got = got.reshape(count, rows, entries)
    hit = lax.broadcasted_iota(jnp.int32, (1, rows, entries), 1) == row_idx[None]
    return jnp.sum(jnp.where(hit, got, 0.0), axis=1)


def unpack(entries, rows, row_idx, hot):
    count, size = entries.shape
    hit = lax.broadcasted_iota(jnp.int32, (1, rows, size), 1) == row_idx[None]
    total = None
    for part in split3(entries):
        spread = jnp.where(hit, part.astype(jnp.float32)[:, None, :], 0.0)
        spread = spread.reshape(count * rows, size).astype(jnp.bfloat16)
        term = lax.dot_general(
            spread, hot, (((1,), (1,)), ((), ())), preferred_element_type=jnp.float32
        )
        total = term if total is None else total + term
    return total


def kernel(
    n_tx,
    n_ty,
    thick_hbm,
    vel_hbm,
    trc_hbm,
    forcing_hbm,
    levels_hbm,
    area_levels_hbm,
    height_hbm,
    transport_hbm,
    send_hbm,
    receive_hbm,
    own_hbm,
    out_vel,
    out_trc,
    out_height,
    out_transport,
    thick_in,
    vel_in,
    trc_in,
    forcing,
    levels,
    area_levels_in,
    height_in,
    transport_in,
    send_in,
    receive_in,
    own_in,
    in_sem,
    coef,
    vel,
    trc,
    low_s,
    inv_s,
    ratio_s,
    val,
    a2a_out,
    a2a_in,
    pair_out,
    right_out,
    left_out,
    pair_in,
    side_in,
    win,
    a2a_send,
    a2a_recv,
    halo_send,
    halo_recv,
):
    tx = lax.axis_index("tx")
    ty = lax.axis_index("ty")
    rows = height_in.shape[0]
    cols = LANES - 2 * HALO
    brows = forcing.shape[1]
    remote = n_tx * LANES
    local = rows * cols

    def present(dx, dy):
        return (tx + dx >= 0) & (tx + dx < n_tx) & (ty + dy >= 0) & (ty + dy < n_ty)

    def fetch(number, src, dst):
        copy = pltpu.make_async_copy(src, dst, in_sem.at[number])
        copy.start()
        return copy

    vel_copy = fetch(0, vel_hbm, vel_in)
    thick_copy = fetch(1, thick_hbm, thick_in)
    level_copy = fetch(2, levels_hbm, levels)
    area_level_copy = fetch(3, area_levels_hbm, area_levels_in)
    forcing_copy = fetch(4, forcing_hbm, forcing)
    send_copy = fetch(5, send_hbm, send_in)
    height_copy = fetch(6, height_hbm, height_in)
    transport_copy = fetch(7, transport_hbm, transport_in)
    trc_copy = fetch(8, trc_hbm, trc_in)
    receive_copy = fetch(9, receive_hbm, receive_in)
    own_copy = fetch(10, own_hbm, own_in)

    barrier = pltpu.get_barrier_semaphore()

    def greet(step, carry):
        pl.semaphore_signal(
            barrier,
            inc=1,
            device_id={"tx": lax.rem(tx + step, n_tx), "ty": ty},
            device_id_type=pl.DeviceIdType.MESH,
        )
        return carry

    a2a_in[...] = jnp.zeros_like(a2a_in)
    pair_in[...] = jnp.zeros_like(pair_in)
    side_in[...] = jnp.zeros_like(side_in)

    lax.fori_loop(1, n_tx, greet, 0)
    for dx, dy in OFFSETS:
        if dy != 0:

            @pl.when(present(dx, dy))
            def _():
                pl.semaphore_signal(
                    barrier,
                    inc=1,
                    device_id={"tx": tx + dx, "ty": ty + dy},
                    device_id_type=pl.DeviceIdType.MESH,
                )

    thick_copy.wait()
    size = coef.shape[1]
    row_at = lax.broadcasted_iota(jnp.int32, (size, LANES), 0)
    lane_at = lax.broadcasted_iota(jnp.int32, (size, LANES), 1)
    row = thick_in[...]
    row = jnp.concatenate([row, jnp.ones((1, LANES - LEV), jnp.float32)], axis=1)

    def along_rows(x):
        column = jnp.sum(jnp.where(row_at == lane_at, x, 0.0), axis=1, keepdims=True)
        return jnp.broadcast_to(column, (size, LANES))

    thick = along_rows(row)
    coef[0] = thick
    def at_level(which, k):
        return jnp.broadcast_to(coef[which, pl.ds(k, 1), :], (brows, LANES))

    def pair(ref, k):
        first = pl.multiple_of(k * 2 * brows, 2 * brows)
        return (
            ref[pl.ds(first, brows, stride=2), :],
            ref[pl.ds(first + 1, brows, stride=2), :],
        )

    def put_pair(ref, k, one, two):
        first = pl.multiple_of(k * 2 * brows, 2 * brows)
        ref[pl.ds(first, brows, stride=2), :] = one
        ref[pl.ds(first + 1, brows, stride=2), :] = two

    def sweep(step, carry, unroll):
        def several(block, inner):
            for sub in range(unroll):
                inner = step(block * unroll + sub, inner)
            return inner

        return lax.fori_loop(0, LEV // unroll, several, carry)

    level_copy.wait()
    lev = levels[...]
    wet0 = lev > 0

    def by_lanes(x):
        return jnp.concatenate([x[r : r + 1] for r in range(x.shape[0])], axis=1)

    def slots(start, size):
        idx = by_lanes(send_in[start // LANES : (start + size) // LANES, :])
        return idx >> 7, one_hot(idx & (LANES - 1))

    def own_slots():
        halves = LANES // cols
        got = [own_in[pl.ds(h, rows // halves, stride=halves), :] for h in range(halves)]
        idx = by_lanes(jnp.concatenate(got, axis=1))
        return idx >> 7, one_hot(idx & (LANES - 1))

    def cell_parts(idx):
        return lax.div(idx + cols, cols) - 1, one_hot(lax.rem(idx + cols, cols))

    def cells(start, size):
        return cell_parts(by_lanes(receive_in[start // LANES : (start + size) // LANES, :]))

    chunk = min(1024, remote)
    per_chunk = chunk // LANES
    chunks = range(0, remote, chunk)

    send_copy.wait()
    slot_maps = [slots(first, chunk) for first in chunks]
    vel_copy.wait()
    vel[...] = vel_in[...].astype(jnp.float32)

    def add_level(k, carry):
        su, sv, depth = carry
        t = at_level(0, k)
        wet = jnp.where(lev > k, t, 0.0)
        uu, vv = pair(vel, k)
        su = su + wet * uu
        sv = sv + wet * vv
        return su, sv, depth + wet

    zero = jnp.zeros((brows, LANES), jnp.float32)
    sum_u, sum_v, depth = sweep(add_level, (zero, zero, zero), 10)
    forcing_copy.wait()
    wind_x = jnp.where(wet0, forcing[0], 0.0)
    wind_y = jnp.where(wet0, forcing[1], 0.0)
    payload = jnp.concatenate([sum_u, sum_v, wind_x, wind_y], axis=0)

    def exchange_copy(stage, peer, mine):
        return pltpu.make_async_remote_copy(
            src_ref=a2a_out.at[stage, peer],
            dst_ref=a2a_in.at[stage, mine],
            send_sem=a2a_send.at[stage, peer],
            recv_sem=a2a_recv.at[stage, mine],
            device_id={"tx": peer, "ty": ty},
            device_id_type=pl.DeviceIdType.MESH,
        )

    def start_exchange(stage):
        def go(step, carry):
            exchange_copy(stage, lax.rem(tx + step, n_tx), tx).start()
            return carry

        lax.fori_loop(1, n_tx, go, 0)

    def finish_exchange(stage):
        def go(step, carry):
            exchange_copy(stage, lax.rem(tx + step, n_tx), tx).wait_send()
            source = lax.rem(tx + step, n_tx)
            exchange_copy(stage, source, source).wait_recv()
            return carry

        lax.fori_loop(1, n_tx, go, 0)

    def stage_out(stage, first, packed):
        for block in range(per_chunk):
            a2a_out[stage, first // LANES + block] = packed[:, block * LANES : (block + 1) * LANES]

    def stage_in(stage, first):
        return jnp.concatenate(
            [a2a_in[stage, first // LANES + block] for block in range(per_chunk)], axis=1
        )

    for first, (row_idx, hot) in zip(chunks, slot_maps):
        stage_out(0, first, pack(payload, 4, row_idx, hot))

    greeted = jnp.int32(n_tx - 1)
    for dx, dy in OFFSETS:
        if dy != 0:
            greeted = greeted + jnp.where(present(dx, dy), 1, 0)
    pl.semaphore_wait(barrier, greeted)
    start_exchange(0)

    lane = lax.broadcasted_iota(jnp.int32, (rows, LANES), 1)

    def halo_copy(stage, dx, dy):
        there = slot_of(-dx, -dy)
        if dy == 0:
            src, dst = pair_out.at[stage], pair_in.at[stage, 2 - dx]
        else:
            src = (right_out if dy > 0 else left_out).at[stage]
            dst = side_in.at[stage, 2 - dx, 0 if dy > 0 else 1]
        return pltpu.make_async_remote_copy(
            src_ref=src,
            dst_ref=dst,
            send_sem=halo_send.at[stage, slot_of(dx, dy)],
            recv_sem=halo_recv.at[stage, there],
            device_id={"tx": tx + dx, "ty": ty + dy},
            device_id_type=pl.DeviceIdType.MESH,
        )

    def start_halo(stage, tiles):
        for half in range(2):
            pair_out[stage, half] = jnp.where(
                lane < cols, tiles[2 * half], pltpu.roll(tiles[2 * half + 1], cols, 1)
            )
        right = jnp.zeros((rows, LANES), jnp.float32)
        left = jnp.zeros((rows, LANES), jnp.float32)
        for f in range(4):
            here = (lane >= HALO * f) & (lane < HALO * (f + 1))
            shift = (HALO * f - (cols - HALO)) % LANES
            right = jnp.where(here, pltpu.roll(tiles[f], shift, 1) if shift else tiles[f], right)
            shift = HALO * f
            left = jnp.where(here, pltpu.roll(tiles[f], shift, 1) if shift else tiles[f], left)
        right_out[stage] = right
        left_out[stage] = left
        for dx, dy in OFFSETS:

            @pl.when(present(dx, dy))
            def _():
                halo_copy(stage, dx, dy).start()

    def roll_lanes(x, shift):
        shift = shift % LANES
        return pltpu.roll(x, shift, 1) if shift else x

    def finish_halo(stage, tiles):
        for dx, dy in OFFSETS:

            @pl.when(present(dx, dy))
            def _():
                halo_copy(stage, dx, dy).wait_send()
                halo_copy(stage, -dx, -dy).wait_recv()

        for dx in (-2, -1, 0, 1, 2):
            from_left = side_in[stage, dx + 2, 0]
            from_right = side_in[stage, dx + 2, 1]
            for f in range(4):
                if dx == 0:
                    middle = roll_lanes(tiles[f], HALO)
                else:
                    pair = pair_in[stage, dx + 2, f // 2]
                    middle = roll_lanes(pair, HALO if f % 2 == 0 else HALO - cols)
                block = jnp.where(
                    lane < HALO,
                    roll_lanes(from_left, -HALO * f),
                    jnp.where(
                        lane >= HALO + cols,
                        roll_lanes(from_right, HALO + cols - HALO * f),
                        middle,
                    ),
                )
                win[stage * 4 + f, (dx + 2) * rows : (dx + 3) * rows, :] = block

    area_level_copy.wait()
    def widen(x):
        return jnp.concatenate([x, jnp.zeros((rows, LANES - cols), x.dtype)], axis=1)

    area_lev = widen(area_levels_in[...])
    def add_area_level(k, area_depth):
        t = jnp.broadcast_to(coef[0, pl.ds(k, 1), :], (rows, LANES))
        return area_depth + jnp.where(area_lev > k, t, 0.0)

    area_depth = sweep(add_area_level, jnp.zeros((rows, LANES), jnp.float32), 10)
    height_copy.wait()
    transport_copy.wait()
    state_tiles = [
        widen(height_in[...]),
        widen(transport_in[0]),
        widen(transport_in[1]),
        area_depth,
    ]
    start_halo(0, state_tiles)

    gap = jnp.where(
        lane_at[:1] < LEV - 1, mixing / (row + pltpu.roll(row, LANES - 1, 1)), 0.0
    )
    coef[1] = along_rows(pltpu.roll(gap, 1, 1)) / thick
    coef[2] = along_rows(gap) / thick

    trc_copy.wait()
    trc[...] = trc_in[...].astype(jnp.float32)
    inv_top = 1.0 / at_level(0, 0)
    heat = jnp.where(wet0, time_step * inv_top * forcing[2], 0.0)
    salt = jnp.where(wet0, time_step * inv_top * forcing[3], 0.0)
    push_x = time_step * inv_top * wind_x
    push_y = time_step * inv_top * wind_y
    tilt = time_step * coriolis

    def top_term(k, x):
        return jnp.where(k == 0, x, 0.0)

    def coefficients(k, ratio):
        low = jnp.where(lev > k, -at_level(1, k), 0.0)
        upp = jnp.where(lev > k + 1, -at_level(2, k), 0.0)
        inv = 1.0 / (1.0 - low - upp - low * ratio)
        ratio = upp * inv
        ratio_s[k] = ratio
        low_s[k] = low * inv
        inv_s[k] = inv
        return ratio

    sweep(coefficients, zero, 6)

    def gather_area():
        total = None
        for first, (row_idx, hot) in zip(chunks, cell_maps):
            term = unpack(stage_in(0, first), rows, row_idx, hot)
            total = term if total is None else total + term
        return total

    own_copy.wait()
    receive_copy.wait()
    own_row, own_hot = own_slots()
    cell_maps = [cells(first, chunk) for first in chunks]
    own_vals = pack(payload, 4, own_row, own_hot)
    cell_row, cell_hot = cell_parts(lax.broadcasted_iota(jnp.int32, (1, local), 1))
    own_area = unpack(own_vals, rows, cell_row, cell_hot)
    finish_exchange(0)
    tile = own_area + gather_area()
    sum_tiles = [tile[f * rows : (f + 1) * rows] for f in range(4)]
    start_halo(1, sum_tiles)

    finish_halo(0, state_tiles)

    def first_forward(k, carry):
        u, v, a, b = carry
        low_inv = low_s[k]
        wet_inv = jnp.where(lev > k, inv_s[k], 0.0)
        uu, vv = pair(vel, k)
        aa, bb = pair(trc, k)
        u = (uu + tilt * vv + top_term(k, push_x)) * wet_inv - low_inv * u
        v = (vv - tilt * uu + top_term(k, push_y)) * wet_inv - low_inv * v
        a = (aa + top_term(k, heat)) * wet_inv - low_inv * a
        b = (bb + top_term(k, salt)) * wet_inv - low_inv * b
        val[0, k] = u
        val[1, k] = v
        val[2, k] = a
        val[3, k] = b
        return u, v, a, b

    sweep(first_forward, (zero,) * 4, 6)

    def first_backward(step, carry):
        k = LEV - 1 - step
        u, v, a, b, du, dv = carry
        ratio = ratio_s[k]
        t = at_level(0, k)
        u = val[0, k] - ratio * u
        v = val[1, k] - ratio * v
        a = val[2, k] - ratio * a
        b = val[3, k] - ratio * b
        val[0, k] = u
        val[1, k] = v
        val[2, k] = a
        val[3, k] = b
        return u, v, a, b, du + t * u, dv + t * v

    mixed = sweep(first_backward, (zero,) * 6, 6)
    first_du, first_dv = mixed[4], mixed[5]

    finish_halo(1, sum_tiles)
    wrows = 5 * rows
    depth_w = win[3]
    rate = transport_rate / LEV
    face_e = jnp.minimum(depth_w, pltpu.roll(depth_w, wrows - 1, 0))
    face_n = jnp.minimum(depth_w, roll_lanes(depth_w, -1))
    filled = depth_w / jnp.maximum(depth_w, depth_floor)
    statics = (rate * face_e, rate * face_n, filled, win[4], win[5], win[6], win[7])
    state = (win[0], roll_lanes(win[0], -1), win[1], win[2])
    shrink = 8
    means = []

    def inner(x):
        return x[shrink : x.shape[0] - shrink]

    for ocean_step in range(STEPS):
        rate_e, rate_n, filled, su, sv, wx, wy = statics
        force_e = coriolis * sv + wx
        force_n = wy - coriolis * su
        push = (rate * force_e, rate * force_n)
        flow_sum = (jnp.zeros_like(force_e), jnp.zeros_like(force_e))
        for part in range(NSUB // shrink):
            rate_e, rate_n = statics[:2]
            push_e, push_n = push
            size = rate_e.shape[0]

            def substep(carry, rate_e=rate_e, rate_n=rate_n, push_e=push_e, push_n=push_n, size=size):
                h, h_next, e, n, te, tn = carry
                e_next = roll_lanes(e, -1)
                h = h - height_rate * (e - pltpu.roll(e, 1, 0) + n - roll_lanes(n, 1))
                h_next = h_next - height_rate * (
                    e_next - pltpu.roll(e_next, 1, 0) + roll_lanes(n, -1) - n
                )
                slope_e = pltpu.roll(h, size - 1, 0) - h
                slope_n = h_next - h
                e = jnp.where(rate_e > 0, e + (push_e - rate_e * slope_e), 0.0)
                n = jnp.where(rate_n > 0, n + (push_n - rate_n * slope_n), 0.0)
                return h, h_next, e, n, te + e, tn + n

            def four(counter, carry, substep=substep):
                return substep(substep(substep(substep(carry))))

            carry = lax.fori_loop(0, shrink // 4, four, state + flow_sum)
            carry = tuple(inner(x) for x in carry)
            statics = tuple(inner(x) for x in statics)
            push = tuple(inner(x) for x in push)
            state, flow_sum = carry[:4], carry[4:]
        mean_e = flow_sum[0] / NSUB
        mean_n = flow_sum[1] / NSUB
        means += [mean_e, mean_n]
        if ocean_step + 1 < STEPS:
            rate_e, rate_n, filled, su, sv, wx, wy = statics
            du = su + time_step * (coriolis * sv + wx)
            dv = sv + time_step * (wy - coriolis * su)
            su = du + (mean_e - du) * filled
            sv = dv + (mean_n - dv) * filled
            statics = (rate_e, rate_n, filled, su, sv, wx, wy)

    def centre(x):
        first = (x.shape[0] - rows) // 2
        return roll_lanes(x[first : first + rows], -HALO)

    flow = jnp.concatenate([centre(x) for x in means], axis=0)
    for first, (row_idx, hot) in zip(chunks, cell_maps):
        stage_out(1, first, pack(flow, 4, row_idx, hot))
    start_exchange(1)
    def second_forward(k, carry):
        u, v, a, b = carry
        low_inv = low_s[k]
        wet_inv = jnp.where(lev > k, inv_s[k], 0.0)
        uu = val[0, k]
        vv = val[1, k]
        u = (uu + tilt * vv + top_term(k, push_x)) * wet_inv - low_inv * u
        v = (vv - tilt * uu + top_term(k, push_y)) * wet_inv - low_inv * v
        a = (val[2, k] + top_term(k, heat)) * wet_inv - low_inv * a
        b = (val[3, k] + top_term(k, salt)) * wet_inv - low_inv * b
        val[0, k] = u
        val[1, k] = v
        val[2, k] = a
        val[3, k] = b
        return u, v, a, b

    sweep(second_forward, (zero,) * 4, 6)

    def second_backward(step, carry):
        k = LEV - 1 - step
        u, v, a, b, du, dv = carry
        ratio = ratio_s[k]
        t = at_level(0, k)
        u = val[0, k] - ratio * u
        v = val[1, k] - ratio * v
        a = val[2, k] - ratio * a
        b = val[3, k] - ratio * b
        val[0, k] = u
        val[1, k] = v
        put_pair(trc, k, a, b)
        return u, v, a, b, du + t * u, dv + t * v

    mixed = sweep(second_backward, (zero,) * 6, 6)
    second_du, second_dv = mixed[4], mixed[5]

    out_trc[...] = trc[...].astype(jnp.bfloat16)
    out_height[...] = centre(state[0])[:, :cols]
    out_transport[0] = centre(state[2])[:, :cols]
    out_transport[1] = centre(state[3])[:, :cols]
    slot_flow = unpack(pack(flow, 4, cell_row, cell_hot), brows, own_row, own_hot)
    finish_exchange(1)
    for first, (row_idx, hot) in zip(chunks, slot_maps):
        slot_flow = slot_flow + unpack(stage_in(1, first), brows, row_idx, hot)

    floor = jnp.maximum(depth, depth_floor)
    shift_u = (slot_flow[0:brows] - first_du) / floor
    shift_v = (slot_flow[brows : 2 * brows] - first_dv) / floor
    carry_u = shift_u + tilt * shift_v
    carry_v = shift_v - tilt * shift_u
    last_u = carry_u + (slot_flow[2 * brows : 3 * brows] - second_du - depth * carry_u) / floor
    last_v = carry_v + (slot_flow[3 * brows :] - second_dv - depth * carry_v) / floor

    def finish(k, carry):
        wet = lev > k
        put_pair(
            vel,
            k,
            val[0, k] + jnp.where(wet, last_u, 0.0),
            val[1, k] + jnp.where(wet, last_v, 0.0),
        )
        return carry

    sweep(finish, 0, 6)
    out_vel[...] = vel[...].astype(jnp.bfloat16)


def deliver(*refs):
    count = (len(refs) - 1) // 2
    sems = refs[-1]
    copies = [
        pltpu.make_async_copy(refs[i], refs[count + i], sems.at[i]) for i in range(count)
    ]
    for copy in copies:
        copy.start()
    for copy in copies:
        copy.wait()


def flat(x, brows):
    x = x.reshape(2, LEV, brows, LANES)
    return jnp.transpose(x, (1, 2, 0, 3)).reshape(LEV * brows * 2, LANES)


def unflat(x, brows):
    x = x.reshape(LEV, brows, 2, LANES)
    return jnp.transpose(x, (2, 0, 1, 3)).reshape(2, LEV, 1, brows * LANES)


def body(
    n_tx,
    n_ty,
    velocity,
    tracers,
    surface_forcing,
    thickness,
    levels,
    surface_levels,
    height,
    transport,
    send_list,
    receive_cell,
    own_slot,
):
    rows, cols = height.shape
    slots = levels.shape[1]
    brows = slots // LANES
    cap = send_list.shape[3]
    forcing = surface_forcing.reshape(4, brows, LANES)
    pad = ((0, 0), (0, 0), (0, LANES - cap))
    sends, receives = send_list[0], receive_cell[0]
    if cap < LANES:
        sends = jnp.pad(sends, pad, constant_values=-1)
        receives = jnp.pad(receives, pad, constant_values=-1)
    operands = (
        thickness.reshape(1, LEV),
        flat(velocity, brows),
        flat(tracers, brows),
        forcing,
        levels.reshape(brows, LANES),
        surface_levels,
        height,
        transport,
        sends[0],
        receives[0],
        own_slot,
    )
    vmem = pl.BlockSpec(memory_space=pltpu.VMEM)
    hbm = pl.BlockSpec(memory_space=pltpu.HBM)
    f32 = jnp.float32
    column = pltpu.VMEM((LEV, brows, LANES), f32)
    whole = (LEV * brows * 2, LANES)
    results = (
        jax.ShapeDtypeStruct(whole, jnp.bfloat16),
        jax.ShapeDtypeStruct(whole, jnp.bfloat16),
        jax.ShapeDtypeStruct((rows, cols), f32),
        jax.ShapeDtypeStruct((2, rows, cols), f32),
    )
    got = pl.pallas_call(
        functools.partial(kernel, n_tx, n_ty),
        out_shape=results,
        in_specs=[hbm] * len(operands),
        out_specs=(vmem,) * 4,
        scratch_shapes=[pltpu.VMEM(x.shape, x.dtype) for x in operands]
        + [
            pltpu.SemaphoreType.DMA((len(operands),)),
            pltpu.VMEM((3, 64, LANES), f32),
            pltpu.VMEM(whole, f32),
            pltpu.VMEM(whole, f32),
            column,
            column,
            column,
            pltpu.VMEM((4, LEV, brows, LANES), f32),
            pltpu.VMEM((2, n_tx, 4, LANES), f32),
            pltpu.VMEM((2, n_tx, 4, LANES), f32),
            pltpu.VMEM((2, 2, rows, LANES), f32),
            pltpu.VMEM((2, rows, LANES), f32),
            pltpu.VMEM((2, rows, LANES), f32),
            pltpu.VMEM((2, 5, 2, rows, LANES), f32),
            pltpu.VMEM((2, 5, 2, rows, LANES), f32),
            pltpu.VMEM((8, 5 * rows, LANES), f32),
            pltpu.SemaphoreType.DMA((2, n_tx)),
            pltpu.SemaphoreType.DMA((2, n_tx)),
            pltpu.SemaphoreType.DMA((2, 15)),
            pltpu.SemaphoreType.DMA((2, 15)),
        ],
        compiler_params=pltpu.CompilerParams(
            collective_id=0, has_side_effects=True, vmem_limit_bytes=48 * 1024 * 1024
        ),
        name="ocean",
    )(*[pltpu.with_memory_space_constraint(x, pltpu.HBM) for x in operands])
    new_vel, new_trc, new_height, new_transport = pl.pallas_call(
        deliver,
        out_shape=results,
        in_specs=[vmem] * 4,
        out_specs=(hbm,) * 4,
        scratch_shapes=[pltpu.SemaphoreType.DMA((4,))],
        name="deliver",
    )(*[pltpu.with_memory_space_constraint(x, pltpu.VMEM) for x in got])
    return (unflat(new_vel, brows), unflat(new_trc, brows), new_height, new_transport)


def solution(mesh):
    in_specs = (
        P(None, None, "ty", "tx"),
        P(None, None, "ty", "tx"),
        P(None, "ty", "tx"),
        P(),
        P("ty", "tx"),
        P("tx", "ty"),
        P("tx", "ty"),
        P(None, "tx", "ty"),
        P("ty", "tx", None, None),
        P("ty", "tx", None, None),
        P("tx", "ty"),
    )
    out_specs = (
        P(None, None, "ty", "tx"),
        P(None, None, "ty", "tx"),
        P("tx", "ty"),
        P(None, "tx", "ty"),
    )
    return jax.shard_map(
        functools.partial(body, mesh.shape["tx"], mesh.shape["ty"]),
        mesh=mesh,
        in_specs=in_specs,
        out_specs=out_specs,
        check_vma=False,
    )
```
